32 devices in a mesh: pipe: 2 (over core), dp: 16 (over z, y, x).
Axes of the slice: x: 2, y: 2, z: 4, core: 2. Of those that a mesh axis runs over, the one named last changes fastest.
Arguments:
- layer_input: bfloat16 [2, 16, 512, 768], P('pipe', 'dp'), may hold values from -100 to 100
- saved_qkv: bfloat16 [2, 16, 512, 2304], P('pipe', 'dp'), may hold values from -27 to 27
- ln_gain: float32 [2, 768], P('pipe'), may hold values from 0.1 to 1.9
- layer_weights: bfloat16 [2, 768, 3072], P('pipe', 'dp'), may hold values from -0.21875 to 0.21875
- rand_blocks: int32 [2, 12, 6, 3], P('pipe'), may hold values from 1 to 6, as said below
- out_grad: bfloat16 [16, 512, 768], P('dp'), may hold values from -6 to 6
Outputs:
- grad_inputs: bfloat16 [2, 16, 512, 768], P('pipe', 'dp')
- grad_weights: float32 [2, 768, 3072], P('pipe', 'dp')
The draws below stay inside these ranges and needn't reach their ends.
Inputs may be any that keep to these rules, and one draw needn't show every extreme that they name: `rand_blocks`: for each layer, head and middle block i (entry i - 1), 3 different blocks other than i - 1, i and i + 1.
All inputs are finite; a program needn't handle non-finite values.
Results may differ from the reference program's by a relative error of at most 0.0072.
Values may be sent and summed in bfloat16 or wider, within the bound.
No kernel may reach another device: no remote copies, remote signals or barrier semaphores. Data moves between devices by JAX's collectives and lax.ppermute only.
A program may use at most 192 MiB of HBM per device.

```python
import math
import jax
import jax.numpy as jnp
from jax import lax

D = 768
HEADS = 12
HEAD_DIM = 64
BLOCK = 64
RAND = 3
NOTE_LEN = 512
LAYERS = 2
NOTES = 16
N_DP = 16


def draw_layer_input(key, part):
    subkeys = jax.random.split(key, 3)
    full_shape = (LAYERS, NOTES, NOTE_LEN, D)
    base_draw = jnp.clip(jax.random.normal(subkeys[0], full_shape, jnp.float32), -4.0, 4.0)
    low_scale, high_scale = (0.3, 3.0)
    column = jnp.exp(jax.random.uniform(subkeys[1], (LAYERS, 1, 1, D), jnp.float32, math.log(low_scale), math.log(high_scale)))
    rowwise = jnp.exp(jax.random.uniform(subkeys[2], (LAYERS, NOTES, NOTE_LEN, 1), jnp.float32, math.log(low_scale), math.log(high_scale)))
    return (base_draw * column * rowwise).astype(jnp.bfloat16)


def draw_saved_qkv(key, part):
    subkeys = jax.random.split(key, 1)
    full_shape = (LAYERS, NOTES, NOTE_LEN, 3, HEADS, HEAD_DIM)
    stacked = jnp.clip(jax.random.normal(subkeys[0], full_shape, jnp.float32), -4.0, 4.0)
    return stacked.reshape(LAYERS, NOTES, NOTE_LEN, 3 * HEADS * HEAD_DIM).astype(jnp.bfloat16)


def draw_rand_blocks(key, part):
    block_count = NOTE_LEN // BLOCK
    candidate = jnp.arange(block_count, dtype=jnp.int32)[None, None, None, :]
    middle = jnp.arange(1, block_count - 1, dtype=jnp.int32)[None, None, :, None]
    allowed = (candidate >= 1) & (candidate <= block_count - 2) & (jnp.abs(candidate - middle) > 1)
    ranking = jax.random.randint(key, (LAYERS, HEADS, block_count - 2, block_count), 0, 1 << 20) * block_count + candidate
    ranking = jnp.where(allowed, ranking, -1)
    unused, chosen = lax.top_k(ranking, RAND)
    return chosen.astype(jnp.int32)


def shard_levels(own_key, dims, cuts, low, high):
    level, own = 1.0, jax.random.fold_in(own_key, 6)
    for axis_at, shards_of in cuts:
        steps = jnp.exp(jax.random.uniform(jax.random.fold_in(own, axis_at), (shards_of,), jnp.float32, low / len(cuts), high / len(cuts)))
        level = level * jnp.repeat(steps, dims[axis_at] // shards_of).reshape([-1 if axis == axis_at else 1 for axis in range(len(dims))])
    return level


def normal_values(own_key, extent, deviation, reach, cuts=(), kind=jnp.bfloat16):
    level = shard_levels(own_key, extent, cuts, -0.22, 0.18) if cuts else 1.0
    array = jax.random.normal(own_key, extent, jnp.float32) * deviation * level
    return jnp.minimum(jnp.maximum(array, -reach), reach).astype(kind)


def setup_inputs(seed: int = 0) -> dict:
    arg_keys = jax.random.split(jax.random.key(seed), 7)
    return {
        "layer_input": draw_layer_input(jax.random.fold_in(arg_keys[6], 71), 0),
        "saved_qkv": draw_saved_qkv(jax.random.fold_in(arg_keys[6], 71), 0),
        "ln_gain": jnp.clip(1.0 + 0.18 * jax.random.normal(arg_keys[2], (LAYERS, D), jnp.float32), 0.1, 1.9),
        "layer_weights": normal_values(arg_keys[3], (LAYERS, D, 4 * HEADS * HEAD_DIM), D ** -0.5, 0.21875, ((0, 2), (1, 16))),
        "rand_blocks": draw_rand_blocks(jax.random.fold_in(arg_keys[6], 71), 0),
        "out_grad": normal_values(arg_keys[5], (NOTES, NOTE_LEN, D), 1.0, 6.0, ((0, 16),)),
    }


EPSILON = 1e-05
NEGATIVE = -1e+30

def normalize(inputs, gain):
    values = inputs.astype(jnp.float32)
    centred = values - lax.optimization_barrier(jnp.mean(values, axis=-1, keepdims=True))
    inverse_std = lax.rsqrt(lax.optimization_barrier(jnp.mean(centred * centred, axis=-1, keepdims=True)) + EPSILON)
    standard = centred * inverse_std
    return ((standard * gain).astype(jnp.bfloat16), standard, inverse_std)

def to_heads(matrix, block_count):
    return matrix.reshape(block_count, BLOCK, HEADS, HEAD_DIM).transpose(2, 0, 1, 3)

def from_heads(tiles):
    head_count, block_count, tile_rows, head_depth = tiles.shape
    return tiles.transpose(1, 2, 0, 3).reshape(block_count * tile_rows, head_count * head_depth)

def key_tables(random_rows):
    head_count, middle_count, draw_count = random_rows.shape
    block_count = middle_count + 2
    middle = jnp.arange(1, block_count - 1, dtype=jnp.int32)
    fixed_rows = jnp.stack([jnp.zeros_like(middle), jnp.full_like(middle, block_count - 1), middle - 1, middle, middle + 1], axis=-1)
    key_table = jnp.concatenate([jnp.broadcast_to(fixed_rows, (head_count, middle_count, 5)), random_rows.astype(jnp.int32)], axis=-1)
    always = middle >= 0
    edge_keep = jnp.stack([always, always, middle != 1, always, middle != block_count - 2], axis=-1)
    keep_mask = jnp.concatenate([edge_keep, jnp.ones((middle_count, draw_count), dtype=jnp.bool_)], axis=-1)
    return (key_table, jnp.repeat(keep_mask, BLOCK, axis=-1))

def softmax_weights(scores):
    largest = lax.optimization_barrier(jnp.max(scores, axis=-1, keepdims=True))
    powers = jnp.exp(scores - largest)
    return (powers / lax.optimization_barrier(jnp.sum(powers, axis=-1, keepdims=True))).astype(jnp.bfloat16)

def product(form, left, right):
    return jnp.einsum(form, left.astype(jnp.float32), right.astype(jnp.float32))

def attend_forward(projected, random_rows):
    length = projected.shape[0]
    block_count = length // BLOCK
    inner_width = HEADS * HEAD_DIM
    queries = to_heads(projected[:, :inner_width], block_count)
    keys_all = to_heads(projected[:, inner_width:2 * inner_width], block_count)
    values_all = to_heads(projected[:, 2 * inner_width:], block_count)
    key_table, keep_mask = key_tables(random_rows)
    head_index = jnp.arange(HEADS)[:, None, None]
    slot_count = key_table.shape[-1]
    key_tiles = keys_all[head_index, key_table].reshape(HEADS, block_count - 2, slot_count * BLOCK, HEAD_DIM)
    value_tiles = values_all[head_index, key_table].reshape(HEADS, block_count - 2, slot_count * BLOCK, HEAD_DIM)
    score_scale = HEAD_DIM ** (-0.5)
    middle_queries = queries[:, 1:block_count - 1]
    scores = product('hmqd,hmjd->hmqj', middle_queries, key_tiles) * score_scale
    scores = jnp.where(keep_mask[None, :, None, :], scores, NEGATIVE)
    middle_weights = softmax_weights(scores)
    global_queries = jnp.stack([queries[:, 0], queries[:, block_count - 1]], axis=1)
    flat_keys = keys_all.reshape(HEADS, length, HEAD_DIM)
    flat_values = values_all.reshape(HEADS, length, HEAD_DIM)
    global_weights = softmax_weights(product('hgqd,hjd->hgqj', global_queries, flat_keys) * score_scale)
    middle_out = product('hmqj,hmjd->hmqd', middle_weights, value_tiles)
    global_out = product('hgqj,hjd->hgqd', global_weights, flat_values)
    context = jnp.concatenate([global_out[:, :1], middle_out, global_out[:, 1:]], axis=1).astype(jnp.bfloat16)
    return (queries, middle_queries, global_queries, key_tiles, value_tiles, flat_keys, flat_values, middle_weights, global_weights, context, key_table)

def attend_backward(grad_context, state):
    queries, middle_queries, global_queries, key_tiles, value_tiles, flat_keys, flat_values, middle_weights, global_weights, context, key_table = state
    block_count = queries.shape[1]
    score_scale = HEAD_DIM ** (-0.5)
    grad_tiles = to_heads(grad_context, block_count)
    row_delta = lax.optimization_barrier(jnp.sum(grad_tiles.astype(jnp.float32) * context.astype(jnp.float32), axis=-1))
    middle_grad = grad_tiles[:, 1:block_count - 1]
    middle_delta = row_delta[:, 1:block_count - 1]
    weight_grad = product('hmqd,hmjd->hmqj', middle_grad, value_tiles)
    score_grad = (middle_weights.astype(jnp.float32) * (weight_grad - middle_delta[..., None])).astype(jnp.bfloat16)
    query_middle = product('hmqj,hmjd->hmqd', score_grad, key_tiles) * score_scale
    key_slots = product('hmqj,hmqd->hmjd', score_grad, middle_queries) * score_scale
    value_slots = product('hmqj,hmqd->hmjd', middle_weights, middle_grad)
    slot_count = key_table.shape[-1]
    tile_shape = (HEADS, block_count - 2, slot_count, BLOCK, HEAD_DIM)
    head_index = jnp.arange(HEADS)[:, None, None]
    key_grad = jnp.zeros(queries.shape, jnp.float32).at[head_index, key_table].add(key_slots.reshape(tile_shape))
    value_grad = jnp.zeros(queries.shape, jnp.float32).at[head_index, key_table].add(value_slots.reshape(tile_shape))
    global_grad = jnp.stack([grad_tiles[:, 0], grad_tiles[:, block_count - 1]], axis=1)
    global_delta = jnp.stack([row_delta[:, 0], row_delta[:, block_count - 1]], axis=1)
    global_weight_grad = product('hgqd,hjd->hgqj', global_grad, flat_values)
    global_score_grad = (global_weights.astype(jnp.float32) * (global_weight_grad - global_delta[..., None])).astype(jnp.bfloat16)
    query_global = product('hgqj,hjd->hgqd', global_score_grad, flat_keys) * score_scale
    key_grad = key_grad + (product('hgqj,hgqd->hjd', global_score_grad, global_queries) * score_scale).reshape(queries.shape)
    value_grad = value_grad + product('hgqj,hgqd->hjd', global_weights, global_grad).reshape(queries.shape)
    query_grad = jnp.concatenate([query_global[:, :1], query_middle, query_global[:, 1:]], axis=1)
    return jnp.concatenate([from_heads(query_grad), from_heads(key_grad), from_heads(value_grad)], axis=-1).astype(jnp.bfloat16)

def layer_backward(upper_grad, standard, inverse_std, gain, weights_full, state):
    inner_width = HEADS * HEAD_DIM
    grad_context = jnp.dot(upper_grad, weights_full[:, 3 * inner_width:], preferred_element_type=jnp.float32).astype(jnp.bfloat16)
    grad_projected = attend_backward(grad_context, state)
    grad_normed = jnp.dot(grad_projected, weights_full[:, :3 * inner_width].T, preferred_element_type=jnp.float32)
    grad_standard = grad_normed * gain
    correction = lax.optimization_barrier(jnp.mean(grad_standard, axis=-1, keepdims=True)) + standard * lax.optimization_barrier(jnp.mean(grad_standard * standard, axis=-1, keepdims=True))
    grad_input = (upper_grad.astype(jnp.float32) + inverse_std * (grad_standard - correction)).astype(jnp.bfloat16)
    return (grad_input, grad_projected)

def reference(layer_input, saved_qkv, ln_gain, layer_weights, rand_blocks, out_grad):
    inner_width = HEADS * HEAD_DIM
    upper_all = out_grad
    input_grads = [None] * LAYERS
    weight_grads = [None] * LAYERS
    for layer in reversed(range(LAYERS)):

        def per_note(running, items):
            note_input, note_projected, note_upper = items
            normed, standard, inverse_std = normalize(note_input, ln_gain[layer])
            state = attend_forward(note_projected, rand_blocks[layer])
            grad_input, grad_projected = layer_backward(note_upper, standard, inverse_std, ln_gain[layer], layer_weights[layer], state)
            context_rows = from_heads(state[9])
            term_rows = jnp.concatenate([jnp.dot(normed.T, grad_projected, preferred_element_type=jnp.float32), jnp.dot(note_upper.T, context_rows, preferred_element_type=jnp.float32)], axis=1)
            return (running + term_rows, grad_input)
        running, grad_all = lax.scan(per_note, jnp.zeros((D, 4 * inner_width), jnp.float32), (layer_input[layer], saved_qkv[layer], upper_all))
        input_grads[layer] = grad_all
        weight_grads[layer] = running / N_DP
        upper_all = grad_all
    return (jnp.stack(input_grads), jnp.stack(weight_grads))
```

```python
import math

import jax
import jax.numpy as jnp
from jax import lax
from jax.experimental import pallas as pl
from jax.experimental.pallas import tpu as pltpu
from jax.sharding import PartitionSpec as P

HEADS = 12
HEAD_DIM = 64
BLOCK = 64
INNER = HEADS * HEAD_DIM
PAIR = 2 * HEAD_DIM
PAIRS = HEADS // 2
EPSILON = 1e-05
NEGATIVE = -1e30
SCALE = HEAD_DIM ** (-0.5)
VMEM_LIMIT = 60 * 1024 * 1024
F32 = jnp.float32
BF16 = jnp.bfloat16
ANY = pl.BlockSpec(memory_space=pl.ANY)
SMEM = pl.BlockSpec(memory_space=pltpu.SMEM)


def dot_nn(left, right):
    return lax.dot_general(left, right, (((1,), (0,)), ((), ())), preferred_element_type=F32)


def dot_nt(left, right):
    return lax.dot_general(left, right, (((1,), (1,)), ((), ())), preferred_element_type=F32)


def dot_tn(left, right):
    return lax.dot_general(left, right, (((0,), (0,)), ((), ())), preferred_element_type=F32)


def call(body, out_shape, in_specs, out_specs, scratch, aliases=None):
    return pl.pallas_call(
        body,
        out_shape=out_shape,
        in_specs=in_specs,
        out_specs=out_specs,
        scratch_shapes=scratch,
        input_output_aliases=aliases or {},
        compiler_params=pltpu.CompilerParams(vmem_limit_bytes=VMEM_LIMIT),
    )


def shape(dims, dtype=BF16):
    return jax.ShapeDtypeStruct(dims, dtype)


def scaled(value):
    return (value.astype(F32) * SCALE).astype(BF16)


def forward_body(skip_ref, q_ref, k_ref, v_ref, weights_ref, context_ref):
    pair = pl.program_id(0)
    length = q_ref.shape[0]
    last = length // BLOCK - 1
    queries = scaled(q_ref[...])
    keys = k_ref[...]
    values_t = v_ref[...].T
    lane = lax.broadcasted_iota(jnp.int32, keys.shape, 1)
    key_block = lax.broadcasted_iota(jnp.int32, (length, length), 0) // BLOCK
    query_block = lax.broadcasted_iota(jnp.int32, (length, length), 1) // BLOCK
    parts = []
    for half in range(2):
        own = (lane >= half * HEAD_DIM) & (lane < (half + 1) * HEAD_DIM)
        scores = dot_nt(jnp.where(own, keys, jnp.zeros_like(keys)), queries)
        low = skip_ref[0, 2 * pair + half]
        high = skip_ref[1, 2 * pair + half]
        masked = ((query_block == 1) & (key_block == low)) | (
            (query_block == last - 1) & (key_block == high)
        )
        scores = jnp.where(masked, NEGATIVE, scores)
        powers = jnp.exp(scores - jnp.max(scores, axis=0, keepdims=True))
        inverse = 1.0 / jnp.sum(powers, axis=0, keepdims=True)
        weights = (powers * inverse).astype(BF16)
        weights_ref[half] = weights
        parts.append(dot_nn(values_t[half * HEAD_DIM : (half + 1) * HEAD_DIM], weights))
    context_ref[...] = jnp.concatenate(parts, axis=0).T.astype(BF16)


def attend_forward(projected, skipped):
    length = projected.shape[0]
    block = (length, PAIR)
    return pl.pallas_call(
        forward_body,
        grid_spec=pltpu.PrefetchScalarGridSpec(
            num_scalar_prefetch=1,
            grid=(PAIRS,),
            in_specs=[
                pl.BlockSpec(block, lambda p, s: (0, p)),
                pl.BlockSpec(block, lambda p, s: (0, PAIRS + p)),
                pl.BlockSpec(block, lambda p, s: (0, 2 * PAIRS + p)),
            ],
            out_specs=[
                pl.BlockSpec((2, length, length), lambda p, s: (p, 0, 0)),
                pl.BlockSpec(block, lambda p, s: (0, p)),
            ],
        ),
        out_shape=(shape((HEADS, length, length)), shape((length, INNER))),
        compiler_params=pltpu.CompilerParams(vmem_limit_bytes=VMEM_LIMIT),
    )(skipped, projected, projected, projected)


def statistics(x):
    values = x.astype(F32)
    centred = values - jnp.mean(values, axis=-1, keepdims=True)
    inverse = lax.rsqrt(jnp.mean(centred * centred, axis=-1, keepdims=True) + EPSILON)
    return centred * inverse, inverse


def norm_body(x_ref, gain_ref, out_ref):
    standard, _ = statistics(x_ref[...])
    out_ref[...] = (standard * gain_ref[...]).astype(BF16).T


def normed_transposed(x, gain):
    length, width = x.shape
    return pl.pallas_call(norm_body, out_shape=shape((width, length)))(x, gain)


def weight_copies(info_ref, pieces, offsets, columns, target, sems, wanted):
    low, high = wanted
    copies = []
    for (first, second), order, (start, stop) in zip(pieces, offsets, columns):
        left, right = max(start, low), min(stop, high)
        if left >= right:
            continue
        half = first.shape[0]
        rows = first.shape[1]
        for slot, offset in enumerate(order):
            source = first if slot < half else second
            row = pl.multiple_of((info_ref[2] ^ offset) * rows, math.gcd(rows, 16))
            copies.append(
                pltpu.make_async_copy(
                    source.at[slot % half, :, pl.ds(left - start, right - left)],
                    target.at[pl.ds(row, rows), pl.ds(left - low, right - left)],
                    sems.at[len(copies)],
                )
            )
    return copies


def attend_body(offsets, columns, aliased, *refs):
    info_ref, received, top, qkv, weights, context = refs[:6]
    chunk_count = len(columns)
    pieces = [(refs[6 + 2 * c], refs[7 + 2 * c]) for c in range(chunk_count)]
    refs = refs[6 + 2 * chunk_count + aliased :]
    grad_out, upper_out = refs[:2]
    upper_v, qkv_v, p_v, context_v, out_w, gc_v, grad_v, base_sems, p_sems, w_sems = refs[2:]

    @pl.when(info_ref[0] == 1)
    def _():
        upper_top = pltpu.make_async_copy(top, upper_v, base_sems.at[0])
        upper_got = pltpu.make_async_copy(received, upper_v, base_sems.at[1])

        @pl.when(info_ref[1] == 1)
        def _():
            upper_top.start()

        @pl.when(info_ref[1] == 0)
        def _():
            upper_got.start()

        w_copies = weight_copies(
            info_ref, pieces, offsets, columns, out_w, w_sems, (3 * INNER, 4 * INNER)
        )
        for copy in w_copies:
            copy.start()
        qkv_copy = pltpu.make_async_copy(qkv, qkv_v, base_sems.at[2])
        context_copy = pltpu.make_async_copy(context, context_v, base_sems.at[3])
        qkv_copy.start()
        context_copy.start()

        def p_copy(pair):
            part = pl.ds(2 * pair, 2)
            return pltpu.make_async_copy(weights.at[part], p_v.at[part], p_sems.at[pair])

        for pair in range(PAIRS):
            p_copy(pair).start()

        @pl.when(info_ref[1] == 1)
        def _():
            upper_top.wait()

        @pl.when(info_ref[1] == 0)
        def _():
            upper_got.wait()

        upper_copy = pltpu.make_async_copy(upper_v, upper_out, base_sems.at[4])
        upper_copy.start()
        for copy in w_copies:
            copy.wait()
        gc_v[...] = dot_nn(upper_v[...], out_w[...]).astype(BF16)
        qkv_copy.wait()
        context_copy.wait()

        def one_pair(pair, carry):
            p_copy(pair).wait()
            base = pl.multiple_of(pair * PAIR, PAIR)
            at = pl.ds(base, PAIR)
            k_at = pl.ds(pl.multiple_of(base + INNER, PAIR), PAIR)
            v_at = pl.ds(pl.multiple_of(base + 2 * INNER, PAIR), PAIR)
            queries = scaled(qkv_v[:, at])
            keys_t = scaled(qkv_v[:, k_at]).T
            values = qkv_v[:, v_at]
            grads = gc_v[:, at]
            lane = lax.broadcasted_iota(jnp.int32, grads.shape, 1)
            zero = jnp.zeros_like(grads)
            product_t = (grads.astype(F32) * context_v[:, at].astype(F32)).T
            key_grad = value_grad = None
            query_parts = []
            for half in range(2):
                rows = slice(half * HEAD_DIM, (half + 1) * HEAD_DIM)
                own = (lane >= half * HEAD_DIM) & (lane < (half + 1) * HEAD_DIM)
                probs = p_v[2 * pair + half]
                delta = jnp.sum(product_t[rows], axis=0, keepdims=True)
                weight_grad = dot_nt(jnp.where(own, values, zero), grads)
                score_grad = (probs.astype(F32) * (weight_grad - delta)).astype(BF16)
                key_part = dot_nn(score_grad, jnp.where(own, queries, zero))
                value_part = dot_nn(probs, jnp.where(own, grads, zero))
                key_grad = key_part if half == 0 else key_grad + key_part
                value_grad = value_part if half == 0 else value_grad + value_part
                query_parts.append(dot_nn(keys_t[rows], score_grad))
            grad_v[:, at] = jnp.concatenate(query_parts, axis=0).T.astype(BF16)
            grad_v[:, k_at] = key_grad.astype(BF16)
            grad_v[:, v_at] = value_grad.astype(BF16)
            return carry

        lax.fori_loop(0, PAIRS, one_pair, 0)
        grad_copy = pltpu.make_async_copy(grad_v, grad_out, base_sems.at[5])
        grad_copy.start()
        upper_copy.wait()
        grad_copy.wait()


def attend_backward(info, received, top, qkv, weights, context, gathered, layout, carry):
    offsets, columns = layout
    length, width = top.shape
    flat = [piece for pair in gathered for piece in pair]
    inputs = [info, received, top, qkv, weights, context] + flat
    aliases = {}
    if carry is not None:
        aliases = {len(inputs): 0, len(inputs) + 1: 1}
        inputs = inputs + list(carry)
    copies = sum(
        len(order) for order, (start, stop) in zip(offsets, columns) if stop > 3 * INNER
    )

    def body(*refs):
        attend_body(offsets, columns, len(aliases), *refs)

    return call(
        body,
        (shape((length, 3 * INNER)), shape((length, width))),
        [SMEM] + [ANY] * (len(inputs) - 1),
        (ANY, ANY),
        [
            pltpu.VMEM((length, width), BF16),
            pltpu.VMEM((length, 3 * INNER), BF16),
            pltpu.VMEM((HEADS, length, length), BF16),
            pltpu.VMEM((length, INNER), BF16),
            pltpu.VMEM((width, INNER), BF16),
            pltpu.VMEM((length, INNER), BF16),
            pltpu.VMEM((length, 3 * INNER), BF16),
            pltpu.SemaphoreType.DMA((6,)),
            pltpu.SemaphoreType.DMA((PAIRS,)),
            pltpu.SemaphoreType.DMA((copies,)),
        ],
        aliases,
    )(*inputs)


def project_body(offsets, columns, aliased, *refs):
    info_ref, gain_ref, upper, grad, x = refs[:5]
    chunk_count = len(columns)
    pieces = [(refs[5 + 2 * c], refs[6 + 2 * c]) for c in range(chunk_count)]
    refs = refs[5 + 2 * chunk_count + aliased :]
    out = refs[0]
    upper_v, grad_v, x_v, w_v, out_v, sems, w_sems = refs[1:]

    @pl.when(info_ref[0] == 1)
    def _():
        copies = weight_copies(info_ref, pieces, offsets, columns, w_v, w_sems, (0, 3 * INNER))
        for index, (source, target) in enumerate(((upper, upper_v), (grad, grad_v), (x, x_v))):
            copies.append(pltpu.make_async_copy(source, target, sems.at[index]))
        for copy in copies:
            copy.start()
        for copy in copies:
            copy.wait()
        grad_standard = dot_nt(grad_v[...], w_v[...]) * gain_ref[...]
        standard, inverse = statistics(x_v[...])
        correction = jnp.mean(grad_standard, axis=-1, keepdims=True) + standard * jnp.mean(
            grad_standard * standard, axis=-1, keepdims=True
        )
        out_v[...] = (
            upper_v[...].astype(F32) + inverse * (grad_standard - correction)
        ).astype(BF16)
        done = pltpu.make_async_copy(out_v, out, sems.at[3])
        done.start()
        done.wait()


def project(info, gain, upper, grad, x, gathered, layout, carry):
    offsets, columns = layout
    length, width = x.shape
    flat = [piece for pair in gathered for piece in pair]
    inputs = [info, gain, upper, grad, x] + flat
    aliases = {}
    if carry is not None:
        aliases = {len(inputs): 0}
        inputs = inputs + [carry]
    copies = sum(
        len(order) for order, (start, stop) in zip(offsets, columns) if start < 3 * INNER
    )

    def body(*refs):
        project_body(offsets, columns, len(aliases), *refs)

    return call(
        body,
        shape((length, width)),
        [SMEM, pl.BlockSpec(memory_space=pltpu.VMEM)] + [ANY] * (len(inputs) - 2),
        ANY,
        [
            pltpu.VMEM((length, width), BF16),
            pltpu.VMEM((length, 3 * INNER), BF16),
            pltpu.VMEM((length, width), BF16),
            pltpu.VMEM((width, 3 * INNER), BF16),
            pltpu.VMEM((length, width), BF16),
            pltpu.SemaphoreType.DMA((4,)),
            pltpu.SemaphoreType.DMA((copies,)),
        ],
        aliases,
    )(*inputs)


def term_body(offsets, columns, *refs):
    info_ref, normed_t, grad, upper, context = refs[:5]
    outs = refs[5 : 5 + 2 * len(columns)]
    normed_v, grad_v, upper_v, context_v, term_v, sems, out_sems = refs[5 + 2 * len(columns) :]
    loads = [
        pltpu.make_async_copy(source, target, sems.at[index])
        for index, (source, target) in enumerate(
            ((normed_t, normed_v), (grad, grad_v), (upper, upper_v), (context, context_v))
        )
    ]
    for load in loads:
        load.start()
    copies = []

    def send(low, high):
        for chunk, ((start, stop), order) in enumerate(zip(columns, offsets)):
            left, right = max(start, low), min(stop, high)
            if left >= right:
                continue
            half = outs[2 * chunk].shape[0]
            rows = outs[2 * chunk].shape[1]
            for slot, offset in enumerate(order):
                target = outs[2 * chunk + (slot >= half)]
                row = pl.multiple_of((info_ref[2] ^ offset) * rows, math.gcd(rows, 16))
                copy = pltpu.make_async_copy(
                    term_v.at[pl.ds(row, rows), pl.ds(left, right - left)],
                    target.at[slot % half, :, pl.ds(left - start, right - left)],
                    out_sems.at[len(copies)],
                )
                copy.start()
                copies.append(copy)

    loads[0].wait()
    loads[1].wait()
    for group in range(3):
        low = group * INNER
        term_v[:, low : low + INNER] = dot_nn(
            normed_v[...], grad_v[:, low : low + INNER]
        ).astype(BF16)
        send(low, low + INNER)
    loads[2].wait()
    loads[3].wait()
    term_v[:, 3 * INNER :] = dot_tn(upper_v[...], context_v[...]).astype(BF16)
    send(3 * INNER, 4 * INNER)
    for copy in copies:
        copy.wait()


def weight_terms(info, normed_t, grad, upper, context, rows, layout):
    offsets, columns = layout
    width, length = normed_t.shape
    count = len(offsets[0])
    outs = tuple(
        shape((count // 2, rows, stop - start)) for start, stop in columns for _ in range(2)
    )
    copies = 0
    for group in range(4):
        for order, (start, stop) in zip(offsets, columns):
            if max(start, group * INNER) < min(stop, (group + 1) * INNER):
                copies += len(order)

    def body(*refs):
        term_body(offsets, columns, *refs)

    return call(
        body,
        outs,
        [SMEM] + [ANY] * 4,
        (ANY,) * len(outs),
        [
            pltpu.VMEM((width, length), BF16),
            pltpu.VMEM((length, 3 * INNER), BF16),
            pltpu.VMEM((length, width), BF16),
            pltpu.VMEM((length, INNER), BF16),
            pltpu.VMEM((width, 4 * INNER), BF16),
            pltpu.SemaphoreType.DMA((4,)),
            pltpu.SemaphoreType.DMA((copies,)),
        ],
    )(info, normed_t, grad, upper, context)


def bit_orders(count):
    bits = [1 << b for b in range(count.bit_length() - 1)]
    if len(bits) < 3:
        return [bits] * 3
    near, far = bits[:3], bits[3:]
    return [far + near[c:] + near[:c] for c in range(3)]


def slot_offsets(order):
    offsets = [0]
    for bit in order:
        offsets = offsets + [offset ^ bit for offset in offsets]
    return offsets


def across(value, bit):
    count = lax.axis_size("dp")
    return lax.ppermute(value, "dp", [(source, source ^ bit) for source in range(count)])


def gather_rows(shard, orders, columns):
    held = [shard[None, :, start:stop] for start, stop in columns]
    final = [None] * len(columns)
    steps = len(orders[0])
    for step in range(steps):
        got = [across(held[c], orders[c][step]) for c in range(len(columns))]
        for c in range(len(columns)):
            if step + 1 == steps:
                final[c] = (held[c], got[c])
            else:
                held[c] = jnp.concatenate([held[c], got[c]], axis=0)
    return final


def scatter_rows(terms, orders, scale):
    chunk_count = len(orders)
    steps = len(orders[0])
    kept = [[terms[2 * c]] for c in range(chunk_count)]
    outgoing = [terms[2 * c + 1] for c in range(chunk_count)]
    for step in reversed(range(steps)):
        got = [across(outgoing[c], orders[c][step]) for c in range(chunk_count)]
        for c in range(chunk_count):
            kept[c].append(got[c])
        if step:
            half = 1 << (step - 1)
            for c in range(chunk_count):
                total = sum(part[half : 2 * half].astype(F32) for part in kept[c])
                outgoing[c] = total.astype(BF16)
    sums = [sum(part[0].astype(F32) for part in kept[c]) * scale for c in range(chunk_count)]
    return jnp.concatenate(sums, axis=-1)


def on_device(layer_input, saved_qkv, ln_gain, layer_weights, rand_blocks, out_grad):
    sections = lax.axis_size("pipe")
    section = lax.axis_index("pipe")
    replicas = lax.axis_size("dp")
    position = lax.axis_index("dp")
    x, qkv, top, shard = layer_input[0, 0], saved_qkv[0, 0], out_grad[0], layer_weights[0]
    rows, total = shard.shape
    orders = bit_orders(replicas)
    chunk = total // len(orders)
    columns = [(c * chunk, (c + 1) * chunk) for c in range(len(orders))]
    layout = ([slot_offsets(order) for order in orders], columns)

    gathered = gather_rows(shard, orders, columns)

    blocks = x.shape[0] // BLOCK
    draws = jnp.sum(rand_blocks[0], axis=-1)
    low_all = sum(range(3, blocks - 1))
    high_all = sum(range(1, blocks - 3))
    skipped = jnp.stack([low_all - draws[:, 0], high_all - draws[:, -1]])
    weights, context = attend_forward(qkv, skipped)
    normed_t = normed_transposed(x, ln_gain)

    is_top = (section == sections - 1).astype(jnp.int32)
    received = top
    carry = grad_input = None
    for turn in range(sections):
        active = (section == sections - 1 - turn).astype(jnp.int32)
        info = jnp.stack([active, is_top, position])
        carry = attend_backward(
            info, received, top, qkv, weights, context, gathered, layout, carry
        )
        if turn + 1 < sections:
            grad_input = project(
                info, ln_gain, carry[1], carry[0], x, gathered, layout, grad_input
            )
            received = lax.ppermute(
                grad_input, "pipe", [(source, source - 1) for source in range(1, sections)]
            )
    grad, upper = carry
    terms = weight_terms(info, normed_t, grad, upper, context, rows, layout)
    summed = scatter_rows(terms, orders, 1.0 / replicas)
    grad_input = project(info, ln_gain, upper, grad, x, gathered, layout, grad_input)
    return (grad_input[None, None], summed[None])


def solution(mesh):
    placed = (
        P("pipe", "dp", None, None),
        P("pipe", "dp", None, None),
        P("pipe", None),
        P("pipe", "dp", None),
        P("pipe", None, None, None),
        P("dp", None, None),
    )
    return jax.shard_map(
        on_device,
        mesh=mesh,
        in_specs=placed,
        out_specs=(P("pipe", "dp", None, None), P("pipe", "dp", None)),
        check_vma=False,
    )
```

```python
import math

import jax
import jax.numpy as jnp
from jax import lax
from jax.experimental import pallas as pl
from jax.experimental.pallas import tpu as pltpu
from jax.sharding import PartitionSpec as P

HEADS = 12
HEAD_DIM = 64
BLOCK = 64
INNER = HEADS * HEAD_DIM
PAIR = 2 * HEAD_DIM
PAIRS = HEADS // 2
EPSILON = 1e-05
NEGATIVE = -1e30
SCALE = HEAD_DIM ** (-0.5)
QKV_COLUMNS = (0, 3 * INNER)
OUT_COLUMNS = (3 * INNER, 4 * INNER)
PARTS = 3
PART_PAIRS = PAIRS // PARTS
PART = PART_PAIRS * PAIR
MEGABYTE = 1024 * 1024
F32 = jnp.float32
BF16 = jnp.bfloat16
ANY = pl.BlockSpec(memory_space=pl.ANY)
SMEM = pl.BlockSpec(memory_space=pltpu.SMEM)
HBM = pl.BlockSpec(memory_space=pltpu.HBM)
VMEM = pl.BlockSpec(memory_space=pltpu.VMEM)


def dot_nn(left, right):
    return lax.dot_general(left, right, (((1,), (0,)), ((), ())), preferred_element_type=F32)


def dot_nt(left, right):
    return lax.dot_general(left, right, (((1,), (1,)), ((), ())), preferred_element_type=F32)


def dot_tn(left, right):
    return lax.dot_general(left, right, (((0,), (0,)), ((), ())), preferred_element_type=F32)


def call(body, out_shape, in_specs, out_specs, scratch, megabytes, aliases=None):
    return pl.pallas_call(
        body,
        out_shape=out_shape,
        in_specs=in_specs,
        out_specs=out_specs,
        scratch_shapes=scratch,
        input_output_aliases=aliases or {},
        compiler_params=pltpu.CompilerParams(vmem_limit_bytes=megabytes * MEGABYTE),
    )


def shape(dims, dtype=BF16):
    return jax.ShapeDtypeStruct(dims, dtype)


def start_all(copies):
    for copy in copies:
        copy.start()
    return copies


def wait_all(copies):
    for copy in copies:
        copy.wait()


def scaled(value):
    return (value.astype(F32) * SCALE).astype(BF16)


def half_lanes(like, half):
    lane = lax.broadcasted_iota(jnp.int32, like.shape, 1)
    return (lane >= half * HEAD_DIM) & (lane < (half + 1) * HEAD_DIM)


def pair_columns(pair, group):
    return pl.ds(pl.multiple_of(group * INNER + pair * PAIR, PAIR), PAIR)


def part_columns(index, group):
    return pl.ds(pl.multiple_of(group * PART + index * PAIR, PAIR), PAIR)


def statistics(x):
    values = x.astype(F32)
    centred = values - jnp.mean(values, axis=-1, keepdims=True)
    inverse = lax.rsqrt(jnp.mean(centred * centred, axis=-1, keepdims=True) + EPSILON)
    return centred * inverse, inverse


def skipped_block(draws, middle, blocks):
    near = range(3, blocks - 1) if middle == 0 else range(1, blocks - 3)
    return sum(near) - jnp.sum(draws[middle : middle + 1], axis=1, keepdims=True)


def forward_pair(pair, index, rand_ref, qkv_v):
    queries = scaled(qkv_v[:, part_columns(index, 0)])
    keys = qkv_v[:, part_columns(index, 1)]
    values_t = qkv_v[:, part_columns(index, 2)].T
    blocks = queries.shape[0] // BLOCK
    row_block = lax.broadcasted_iota(jnp.int32, queries.shape, 0) // BLOCK
    lane = lax.broadcasted_iota(jnp.int32, queries.shape, 1)
    probs, parts = [], []
    for half in range(2):
        own = half_lanes(keys, half)
        low = skipped_block(rand_ref[2 * pair + half], 0, blocks)
        high = skipped_block(rand_ref[2 * pair + half], blocks - 3, blocks)
        first = (1 - half) * HEAD_DIM
        marks = ((lane == first) & (row_block == low)) | (
            (lane == first + 1) & (row_block == high)
        )
        bars = ((lane == first) & (row_block == 1)) | (
            (lane == first + 1) & (row_block == blocks - 2)
        )
        key_side = jnp.where(own, keys, jnp.where(marks, 1.0, 0.0).astype(BF16))
        query_side = jnp.where(own, queries, jnp.where(bars, NEGATIVE, 0.0).astype(BF16))
        scores = dot_nt(key_side, query_side)
        powers = jnp.exp(scores - jnp.max(scores, axis=0, keepdims=True))
        inverse = 1.0 / jnp.sum(powers, axis=0, keepdims=True)
        weights = (powers * inverse).astype(BF16)
        probs.append(weights)
        parts.append(dot_nn(values_t[half * HEAD_DIM : (half + 1) * HEAD_DIM], weights))
    return probs, jnp.concatenate(parts, axis=0).T.astype(BF16)


def is_top():
    return lax.axis_index("pipe") == lax.axis_size("pipe") - 1


def forward_body(part, aliased, rand_ref, qkv, *refs):
    @pl.when(is_top() if aliased else jnp.logical_not(is_top()))
    def _():
        forward_part(part, bool(aliased), rand_ref, qkv, *refs[aliased:])


def forward_part(part, unroll, rand_ref, qkv, weights, context, kept, qkv_v, p_v, context_v, sems):
    loads = []
    for group in range(3):
        source = qkv.at[:, pl.ds(group * INNER + part * PART, PART)]
        target = qkv_v.at[:, pl.ds(group * PART, PART)]
        loads.append(pltpu.make_async_copy(source, target, sems.at[group]))
    wait_all(start_all(loads))
    stores = start_all([pltpu.make_async_copy(qkv_v, kept, sems.at[3])])

    def p_copy(index):
        at = pl.ds(2 * index, 2)
        return pltpu.make_async_copy(p_v.at[at], weights.at[at], sems.at[5 + index])

    def one_pair(index, unused):
        pair = part * PART_PAIRS + index
        probs, context_part = forward_pair(pair, index, rand_ref, qkv_v)
        for half in range(2):
            p_v[2 * index + half] = probs[half]
        context_v[:, part_columns(index, 0)] = context_part
        p_copy(index).start()
        return unused

    lax.fori_loop(0, PART_PAIRS, one_pair, 0, unroll=unroll)
    stores += start_all([pltpu.make_async_copy(context_v, context, sems.at[4])])
    stores += [p_copy(index) for index in range(PART_PAIRS)]
    wait_all(stores)


def forward(part, rand, qkv, carry):
    length = qkv.shape[0]
    heads = 2 * PART_PAIRS
    carry = list(carry or ())
    aliases = {2 + index: index for index in range(len(carry))}

    def body(*refs):
        forward_body(part, len(carry), *refs)

    return call(
        body,
        (shape((heads, length, length)), shape((length, PART)), shape((length, 3 * PART))),
        [VMEM, HBM] + [ANY] * len(carry),
        (ANY,) * 3,
        [
            pltpu.VMEM((length, 3 * PART), BF16),
            pltpu.VMEM((heads, length, length), BF16),
            pltpu.VMEM((length, PART), BF16),
            pltpu.SemaphoreType.DMA((5 + PART_PAIRS,)),
        ],
        14,
        aliases,
    )(rand, qkv, *carry)


def statistics(x):
    values = x.astype(F32)
    centred = values - jnp.mean(values, axis=-1, keepdims=True)
    inverse = lax.rsqrt(jnp.mean(centred * centred, axis=-1, keepdims=True) + EPSILON)
    return centred * inverse, inverse


def norm_body(x_ref, gain_ref, out_ref):
    standard, _ = statistics(x_ref[...])
    out_ref[...] = (standard * gain_ref[...]).astype(BF16).T


def normed_transposed(x, gain):
    length, width = x.shape
    return call(norm_body, shape((width, length)), [VMEM, VMEM], VMEM, [], 10)(x, gain)


def weight_copies(pieces, layout, target, sems, wanted):
    low, high = wanted
    position = lax.axis_index("dp")
    copies = []
    for (first, second), order, (start, stop) in zip(pieces, *layout):
        left, right = max(start, low), min(stop, high)
        if left >= right:
            continue
        half = first.shape[0]
        rows = first.shape[1]
        for slot, offset in enumerate(order):
            source = first if slot < half else second
            row = pl.multiple_of((position ^ offset) * rows, math.gcd(rows, 16))
            copies.append(
                pltpu.make_async_copy(
                    source.at[slot % half, :, pl.ds(left - start, right - left)],
                    target.at[pl.ds(row, rows), pl.ds(left - low, right - left)],
                    sems.at[len(copies)],
                )
            )
    return copies


def copy_count(layout, wanted):
    return sum(
        len(order)
        for order, (start, stop) in zip(*layout)
        if max(start, wanted[0]) < min(stop, wanted[1])
    )


def is_turn(turn):
    return lax.axis_index("pipe") == lax.axis_size("pipe") - 1 - turn


def zip_pieces(refs, layout):
    count = 2 * len(layout[1])
    return list(zip(refs[:count:2], refs[1:count:2])), refs[count:]


def flat_pieces(gathered):
    return [piece for pair in gathered for piece in pair]


def context_gradient_body(layout, turn, aliased, *refs):
    received, top = refs[:2]
    pieces, refs = zip_pieces(refs[2:], layout)
    gc_out, upper_out, upper_v, out_w, gc_v, sems, w_sems = refs[aliased:]

    @pl.when(is_turn(turn))
    def _():
        w_copies = start_all(weight_copies(pieces, layout, out_w, w_sems, OUT_COLUMNS))

        @pl.when(is_top())
        def _():
            upper_v[...] = top[...]

        @pl.when(jnp.logical_not(is_top()))
        def _():
            upper_v[...] = received[...]

        stores = start_all([pltpu.make_async_copy(upper_v, upper_out, sems.at[0])])
        wait_all(w_copies)
        gc_v[...] = dot_nn(upper_v[...], out_w[...]).astype(BF16)
        stores += start_all([pltpu.make_async_copy(gc_v, gc_out, sems.at[1])])
        wait_all(stores)


def context_gradient(turn, received, top, gathered, layout, carry):
    length, width = top.shape
    inputs = [received, top] + flat_pieces(gathered)
    aliases = {}
    if carry is not None:
        aliases = {len(inputs): 1}
        inputs = inputs + [carry]

    def body(*refs):
        context_gradient_body(layout, turn, len(aliases), *refs)

    return call(
        body,
        (shape((length, INNER)), shape((length, width))),
        [VMEM, VMEM] + [ANY] * (len(inputs) - 2),
        (ANY, ANY),
        [
            pltpu.VMEM((length, width), BF16),
            pltpu.VMEM((width, INNER), BF16),
            pltpu.VMEM((length, INNER), BF16),
            pltpu.SemaphoreType.DMA((2,)),
            pltpu.SemaphoreType.DMA((copy_count(layout, OUT_COLUMNS),)),
        ],
        10,
        aliases,
    )(*inputs)


def backward_pair(pair, index, qkv_v, p_v, context_v, gc_v, grad_v):
    queries = scaled(qkv_v[:, part_columns(index, 0)])
    keys_t = scaled(qkv_v[:, part_columns(index, 1)]).T
    values = qkv_v[:, part_columns(index, 2)]
    grads = gc_v[:, pair_columns(pair, 0)]
    zero = jnp.zeros_like(grads)
    product_t = (grads.astype(F32) * context_v[:, part_columns(index, 0)].astype(F32)).T
    key_grad = value_grad = None
    query_parts = []
    for half in range(2):
        rows = slice(half * HEAD_DIM, (half + 1) * HEAD_DIM)
        own = half_lanes(grads, half)
        probs = p_v[2 * index + half]
        delta = jnp.sum(product_t[rows], axis=0, keepdims=True)
        weight_grad = dot_nt(jnp.where(own, values, zero), grads)
        score_grad = (probs.astype(F32) * (weight_grad - delta)).astype(BF16)
        key_part = dot_nn(score_grad, jnp.where(own, queries, zero))
        value_part = dot_nn(probs, jnp.where(own, grads, zero))
        key_grad = key_part if half == 0 else key_grad + key_part
        value_grad = value_part if half == 0 else value_grad + value_part
        query_parts.append(dot_nn(keys_t[rows], score_grad))
    grad_v[:, part_columns(index, 0)] = jnp.concatenate(query_parts, axis=0).T.astype(BF16)
    grad_v[:, part_columns(index, 1)] = key_grad.astype(BF16)
    grad_v[:, part_columns(index, 2)] = value_grad.astype(BF16)


def attend_body(part, turn, aliased, gc, qkv, weights, context, *refs):
    grad_out, grad_v, sems = refs[aliased:]

    @pl.when(is_turn(turn))
    def _():
        def one_pair(index, unused):
            pair = part * PART_PAIRS + index
            backward_pair(pair, index, qkv, weights, context, gc, grad_v)
            return unused

        lax.fori_loop(0, PART_PAIRS, one_pair, 0, unroll=True)
        wait_all(start_all([pltpu.make_async_copy(grad_v, grad_out, sems.at[0])]))


def attend_backward(part, turn, gc, qkv, weights, context, carry):
    length = gc.shape[0]
    inputs = [gc, qkv, weights, context]
    aliases = {}
    if carry is not None:
        aliases = {4: 0}
        inputs = inputs + [carry]

    def body(*refs):
        attend_body(part, turn, len(aliases), *refs)

    return call(
        body,
        shape((length, 3 * PART)),
        [VMEM] * 4 + [ANY] * (len(inputs) - 4),
        ANY,
        [pltpu.VMEM((length, 3 * PART), BF16), pltpu.SemaphoreType.DMA((1,))],
        14,
        aliases,
    )(*inputs)


def join_parts(grads, target):
    for part, grad in enumerate(grads):
        for group in range(3):
            start = group * INNER + part * PART
            target[:, start : start + PART] = grad[:, group * PART : (group + 1) * PART]


def input_gradient(upper_v, grad_v, x_v, w_v, gain_ref):
    grad_standard = dot_nt(grad_v[...], w_v[...]) * gain_ref[...]
    standard, inverse = statistics(x_v[...])
    correction = jnp.mean(grad_standard, axis=-1, keepdims=True) + standard * jnp.mean(
        grad_standard * standard, axis=-1, keepdims=True
    )
    return (upper_v[...].astype(F32) + inverse * (grad_standard - correction)).astype(BF16)


def project_body(layout, turn, aliased, gain_ref, upper, x, *refs):
    grads, refs = refs[:PARTS], refs[PARTS:]
    pieces, refs = zip_pieces(refs, layout)
    out, w_v, grad_v, out_v, sems, w_sems = refs[aliased:]

    @pl.when(is_turn(turn))
    def _():
        copies = start_all(weight_copies(pieces, layout, w_v, w_sems, QKV_COLUMNS))
        join_parts(grads, grad_v)
        wait_all(copies)
        out_v[...] = input_gradient(upper, grad_v, x, w_v, gain_ref)
        wait_all(start_all([pltpu.make_async_copy(out_v, out, sems.at[0])]))


def project(turn, gain, upper, x, grads, gathered, layout, carry):
    length, width = x.shape
    inputs = [gain, upper, x, *grads]
    count = len(inputs)
    inputs = inputs + flat_pieces(gathered)
    aliases = {}
    if carry is not None:
        aliases = {len(inputs): 0}
        inputs = inputs + [carry]

    def body(*refs):
        project_body(layout, turn, len(aliases), *refs)

    return call(
        body,
        shape((length, width)),
        [VMEM] * count + [ANY] * (len(inputs) - count),
        ANY,
        [
            pltpu.VMEM((width, 3 * INNER), BF16),
            pltpu.VMEM((length, 3 * INNER), BF16),
            pltpu.VMEM((length, width), BF16),
            pltpu.SemaphoreType.DMA((1,)),
            pltpu.SemaphoreType.DMA((copy_count(layout, QKV_COLUMNS),)),
        ],
        18,
        aliases,
    )(*inputs)


def term_body(layout, rows, normed, upper, *refs):
    position = lax.axis_index("dp")
    grads, contexts, refs = refs[:PARTS], refs[PARTS : 2 * PARTS], refs[2 * PARTS :]
    count = 2 * len(layout[1])
    outs, (grad_v, upper_t, normed_v, upper_v) = refs[:count], refs[count:]
    join_parts(grads, grad_v)
    upper_t[...] = upper[...].T
    for chunk, (order, (start, stop)) in enumerate(zip(*layout)):
        half = len(order) // 2
        for slot, offset in enumerate(order):
            row = pl.multiple_of((position ^ offset) * rows, math.gcd(rows, 16))
            own, source = pl.ds(slot * rows, rows), pl.ds(row, rows)
            if start < 3 * INNER:
                normed_v[own] = normed[source]
            if stop > 3 * INNER:
                upper_v[own] = upper_t[source]
        for out, side in ((outs[2 * chunk + 1], 1), (outs[2 * chunk], 0)):
            at = slice(side * half * rows, (side + 1) * half * rows)

            def store(value, low, high, out=out):
                out[:, :, low - start : high - start] = value.astype(BF16).reshape(
                    half, rows, high - low
                )

            if start < 3 * INNER:
                high = min(stop, 3 * INNER)
                store(dot_nn(normed_v[at], grad_v[:, start:high]), start, high)
            for part, context in enumerate(contexts):
                base = 3 * INNER + part * PART
                low, high = max(start, base), min(stop, base + PART)
                if low < high:
                    value = dot_nn(upper_v[at], context[:, low - base : high - base])
                    store(value, low, high)


def weight_terms(normed, upper, grads, contexts, rows, layout):
    width, length = normed.shape
    inputs = [normed, upper, *grads, *contexts]
    orders, columns = layout
    count = len(orders[0])
    outs = tuple(
        shape((count // 2, rows, stop - start)) for start, stop in columns for _ in range(2)
    )

    def body(*refs):
        term_body(layout, rows, *refs)

    return call(
        body,
        outs,
        [VMEM] * len(inputs),
        (VMEM,) * len(outs),
        [
            pltpu.VMEM((length, 3 * INNER), BF16),
            pltpu.VMEM((width, length), BF16),
            pltpu.VMEM((width, length), BF16),
            pltpu.VMEM((width, length), BF16),
        ],
        24,
    )(*inputs)


def bit_orders(count, free):
    bits = [1 << b for b in range(count.bit_length() - 1)]
    near, far = bits[:free], bits[free:][::-1]
    return [far + near[c:] + near[:c] for c in range(free)]


def slot_offsets(order):
    offsets = [0]
    for bit in order:
        offsets = offsets + [offset ^ bit for offset in offsets]
    return offsets


def exchange_layout(total, orders):
    wide = total // len(orders)
    columns = [(c * wide, (c + 1) * wide) for c in range(len(orders))]
    return [slot_offsets(order) for order in orders], columns


def across(value, bit):
    count = lax.axis_size("dp")
    return lax.ppermute(value, "dp", [(source, source ^ bit) for source in range(count)])


class Gather:
    def __init__(self, shard, orders):
        self.orders = orders
        self.steps = len(orders[0])
        self.layout = exchange_layout(shard.shape[1], orders)
        self.held = [shard[None]]
        self.step = 0
        self.final = None

    def advance(self):
        step, chunks = self.step, len(self.orders)
        if len(self.held) == 1 and len({order[step] for order in self.orders}) > 1:
            self.held = [self.held[0][:, :, start:stop] for start, stop in self.layout[1]]
        got = [across(held, order[step]) for held, order in zip(self.held, self.orders)]
        self.step = step + 1
        if self.step < self.steps:
            self.held = [jnp.concatenate(pair, axis=0) for pair in zip(self.held, got)]
        else:
            if len(got) < chunks:
                self.held = [self.held[0][:, :, start:stop] for start, stop in self.layout[1]]
                got = [got[0][:, :, start:stop] for start, stop in self.layout[1]]
            self.final = list(zip(self.held, got))

    def after(self, *values):
        self.held, values = lax.optimization_barrier((self.held, values))
        return values


def scatter_rows(terms, orders, scale):
    chunk_count = len(orders)
    steps = len(orders[0])
    kept = [[terms[2 * c]] for c in range(chunk_count)]
    outgoing = [terms[2 * c + 1] for c in range(chunk_count)]
    for step in reversed(range(steps)):
        if step == 0 and all(order[0] == orders[0][0] for order in orders):
            break
        got = [across(outgoing[c], orders[c][step]) for c in range(chunk_count)]
        for c in range(chunk_count):
            kept[c].append(got[c])
        if step:
            half = 1 << (step - 1)
            for c in range(chunk_count):
                total = sum(part[half : 2 * half].astype(F32) for part in kept[c])
                outgoing[c] = total.astype(BF16)
    total = jnp.concatenate(
        [sum(part[0].astype(F32) for part in kept[c]) for c in range(chunk_count)], axis=-1
    )
    if len(kept[0]) <= steps:
        last = across(jnp.concatenate([out[0] for out in outgoing], axis=-1), orders[0][0])
        total = total + last.astype(F32)
    return total * scale


def on_device(layer_input, saved_qkv, ln_gain, layer_weights, rand_blocks, out_grad):
    sections = lax.axis_size("pipe")
    replicas = lax.axis_size("dp")
    x, qkv, top, shard = layer_input[0, 0], saved_qkv[0, 0], out_grad[0], layer_weights[0]
    rand = rand_blocks[0]
    rows, total = shard.shape

    orders = bit_orders(replicas, 3)
    gather = Gather(shard, orders)
    saved = [forward(part, rand, qkv, None) for part in range(PARTS)]
    saved = list(gather.after(*saved))
    gather.advance()
    for part in range(PARTS):
        saved[part] = forward(part, rand, qkv, saved[part])
        if part + 1 < PARTS:
            (saved[part],) = gather.after(saved[part])
            gather.advance()
            if part == 0:
                gather.advance()
    while gather.final is None:
        gather.advance()
    normed = normed_transposed(x, ln_gain)

    received = top
    upper = grad_input = None
    grads = [None] * PARTS
    for turn in range(sections):
        gc, upper = context_gradient(turn, received, top, gather.final, gather.layout, upper)
        for part in range(PARTS):
            weights, context, columns = saved[part]
            grads[part] = attend_backward(
                part, turn, gc, columns, weights, context, grads[part]
            )
        if turn + 1 < sections:
            grad_input = project(
                turn, ln_gain, upper, x, grads, gather.final, gather.layout, grad_input
            )
            received = lax.ppermute(
                grad_input, "pipe", [(source, source - 1) for source in range(1, sections)]
            )
    contexts = [context for _, context, _ in saved]
    terms = weight_terms(normed, upper, grads, contexts, rows, exchange_layout(total, orders))
    summed = scatter_rows(terms, orders, 1.0 / replicas)
    grad_input = project(
        sections - 1, ln_gain, upper, x, grads, gather.final, gather.layout, grad_input
    )
    return (grad_input[None, None], summed[None])


def solution(mesh):
    placed = (
        P("pipe", "dp", None, None),
        P("pipe", "dp", None, None),
        P("pipe", None),
        P("pipe", "dp", None),
        P("pipe", None, None, None),
        P("dp", None, None),
    )
    return jax.shard_map(
        on_device,
        mesh=mesh,
        in_specs=placed,
        out_specs=(P("pipe", "dp", None, None), P("pipe", "dp", None)),
        check_vma=False,
    )
```

```python
import math

import jax
import jax.numpy as jnp
from jax import lax
from jax.experimental import pallas as pl
from jax.experimental.pallas import tpu as pltpu
from jax.sharding import PartitionSpec as P

HEADS = 12
HEAD_DIM = 64
BLOCK = 64
INNER = HEADS * HEAD_DIM
PAIR = 2 * HEAD_DIM
PAIRS = HEADS // 2
EPSILON = 1e-05
NEGATIVE = -1e30
SCALE = HEAD_DIM ** (-0.5)
QKV_COLUMNS = (0, 3 * INNER)
OUT_COLUMNS = (3 * INNER, 4 * INNER)
MEGABYTE = 1024 * 1024
F32 = jnp.float32
BF16 = jnp.bfloat16
ANY = pl.BlockSpec(memory_space=pl.ANY)
SMEM = pl.BlockSpec(memory_space=pltpu.SMEM)
HBM = pl.BlockSpec(memory_space=pltpu.HBM)
VMEM = pl.BlockSpec(memory_space=pltpu.VMEM)


def dot_nn(left, right):
    return lax.dot_general(left, right, (((1,), (0,)), ((), ())), preferred_element_type=F32)


def dot_nt(left, right):
    return lax.dot_general(left, right, (((1,), (1,)), ((), ())), preferred_element_type=F32)


def dot_tn(left, right):
    return lax.dot_general(left, right, (((0,), (0,)), ((), ())), preferred_element_type=F32)


def call(body, out_shape, in_specs, out_specs, scratch, megabytes, aliases=None):
    return pl.pallas_call(
        body,
        out_shape=out_shape,
        in_specs=in_specs,
        out_specs=out_specs,
        scratch_shapes=scratch,
        input_output_aliases=aliases or {},
        compiler_params=pltpu.CompilerParams(vmem_limit_bytes=megabytes * MEGABYTE),
    )


def shape(dims, dtype=BF16):
    return jax.ShapeDtypeStruct(dims, dtype)


def start_all(copies):
    for copy in copies:
        copy.start()
    return copies


def wait_all(copies):
    for copy in copies:
        copy.wait()


def scaled(value):
    return (value.astype(F32) * SCALE).astype(BF16)


def half_lanes(like, half):
    lane = lax.broadcasted_iota(jnp.int32, like.shape, 1)
    return (lane >= half * HEAD_DIM) & (lane < (half + 1) * HEAD_DIM)


def columns_of(pair, group, width):
    return pl.ds(pl.multiple_of(group * width + pair * PAIR, PAIR), PAIR)


def skipped_block(draws, middle, blocks):
    near = range(3, blocks - 1) if middle == 0 else range(1, blocks - 3)
    return sum(near) - jnp.sum(draws[middle : middle + 1], axis=1, keepdims=True)


def forward_pair(pair, index, width, rand_ref, qkv_v):
    queries = scaled(qkv_v[:, columns_of(index, 0, width)])
    keys = qkv_v[:, columns_of(index, 1, width)]
    values_t = qkv_v[:, columns_of(index, 2, width)].T
    blocks = queries.shape[0] // BLOCK
    row_block = lax.broadcasted_iota(jnp.int32, queries.shape, 0) // BLOCK
    lane = lax.broadcasted_iota(jnp.int32, queries.shape, 1)
    probs, parts = [], []
    for half in range(2):
        own = half_lanes(keys, half)
        low = skipped_block(rand_ref[2 * pair + half], 0, blocks)
        high = skipped_block(rand_ref[2 * pair + half], blocks - 3, blocks)
        first = (1 - half) * HEAD_DIM
        marks = ((lane == first) & (row_block == low)) | (
            (lane == first + 1) & (row_block == high)
        )
        bars = ((lane == first) & (row_block == 1)) | (
            (lane == first + 1) & (row_block == blocks - 2)
        )
        key_side = jnp.where(own, keys, jnp.where(marks, 1.0, 0.0).astype(BF16))
        query_side = jnp.where(own, queries, jnp.where(bars, NEGATIVE, 0.0).astype(BF16))
        scores = dot_nt(key_side, query_side)
        powers = jnp.exp(scores - jnp.max(scores, axis=0, keepdims=True))
        inverse = 1.0 / jnp.sum(powers, axis=0, keepdims=True)
        weights = (powers * inverse).astype(BF16)
        probs.append(weights)
        parts.append(dot_nn(values_t[half * HEAD_DIM : (half + 1) * HEAD_DIM], weights))
    return probs, jnp.concatenate(parts, axis=0).T.astype(BF16)


def is_top():
    return lax.axis_index("pipe") == lax.axis_size("pipe") - 1


def forward_body(pairs, aliased, rand_ref, qkv, *refs):
    @pl.when(is_top() if aliased else jnp.logical_not(is_top()))
    def _():
        forward_part(pairs, rand_ref, qkv, *refs[aliased:])


def forward_part(pairs, rand_ref, qkv, weights, context, kept, qkv_v, p_v, context_v, sems):
    first, count = pairs
    width = count * PAIR
    loads, stores = [], []
    for group in range(3):
        at = pl.ds(group * INNER + first * PAIR, width)
        held = qkv_v.at[:, pl.ds(group * width, width)]
        loads.append(pltpu.make_async_copy(qkv.at[:, at], held, sems.at[group]))
        stores.append(pltpu.make_async_copy(held, kept.at[:, at], sems.at[3 + group]))
    wait_all(start_all(loads))
    start_all(stores)

    def p_copy(index):
        held, at = pl.ds(2 * index, 2), pl.ds(2 * (first + index), 2)
        return pltpu.make_async_copy(p_v.at[held], weights.at[at], sems.at[7 + index])

    def one_pair(index, unused):
        probs, context_part = forward_pair(first + index, index, width, rand_ref, qkv_v)
        for half in range(2):
            p_v[2 * index + half] = probs[half]
        context_v[:, columns_of(index, 0, width)] = context_part
        p_copy(index).start()
        return unused

    lax.fori_loop(0, count, one_pair, 0)
    target = context.at[:, pl.ds(first * PAIR, width)]
    stores += start_all([pltpu.make_async_copy(context_v, target, sems.at[6])])
    stores += [p_copy(index) for index in range(count)]
    wait_all(stores)


def forward(pairs, rand, qkv, carry):
    first, count = pairs
    length = qkv.shape[0]
    carry = list(carry or ())
    aliases = {2 + index: index for index in range(len(carry))}

    def body(*refs):
        forward_body(pairs, len(carry), *refs)

    return call(
        body,
        (shape((HEADS, length, length)), shape((length, INNER)), shape((length, 3 * INNER))),
        [VMEM, HBM] + [ANY] * len(carry),
        (ANY,) * 3,
        [
            pltpu.VMEM((length, 3 * PAIR * count), BF16),
            pltpu.VMEM((2 * count, length, length), BF16),
            pltpu.VMEM((length, PAIR * count), BF16),
            pltpu.SemaphoreType.DMA((7 + count,)),
        ],
        22 if count > 2 else 14,
        aliases,
    )(rand, qkv, *carry)


def statistics(x):
    values = x.astype(F32)
    centred = values - jnp.mean(values, axis=-1, keepdims=True)
    inverse = lax.rsqrt(jnp.mean(centred * centred, axis=-1, keepdims=True) + EPSILON)
    return centred * inverse, inverse


def norm_body(x_ref, gain_ref, out_ref):
    standard, _ = statistics(x_ref[...])
    out_ref[...] = (standard * gain_ref[...]).astype(BF16).T


def normed_transposed(x, gain):
    length, width = x.shape
    return call(norm_body, shape((width, length)), [VMEM, VMEM], VMEM, [], 10)(x, gain)


def weight_copies(pieces, layout, target, sems, wanted):
    low, high = wanted
    position = lax.axis_index("dp")
    copies = []
    for (first, second), order, (start, stop) in zip(pieces, *layout):
        left, right = max(start, low), min(stop, high)
        if left >= right:
            continue
        half = first.shape[0]
        rows = first.shape[1]
        for slot, offset in enumerate(order):
            source = first if slot < half else second
            row = pl.multiple_of((position ^ offset) * rows, math.gcd(rows, 16))
            copies.append(
                pltpu.make_async_copy(
                    source.at[slot % half, :, pl.ds(left - start, right - left)],
                    target.at[pl.ds(row, rows), pl.ds(left - low, right - left)],
                    sems.at[len(copies)],
                )
            )
    return copies


def copy_count(layout, wanted):
    return sum(
        len(order)
        for order, (start, stop) in zip(*layout)
        if max(start, wanted[0]) < min(stop, wanted[1])
    )


def is_turn(turn):
    return lax.axis_index("pipe") == lax.axis_size("pipe") - 1 - turn


def zip_pieces(refs, layout):
    count = 2 * len(layout[1])
    return list(zip(refs[:count:2], refs[1:count:2])), refs[count:]


def flat_pieces(gathered):
    return [piece for pair in gathered for piece in pair]


def backward_pair(pair, qkv_v, p_v, context_v, gc_v, grad_v):
    queries = scaled(qkv_v[:, columns_of(pair, 0, INNER)])
    keys_t = scaled(qkv_v[:, columns_of(pair, 1, INNER)]).T
    values = qkv_v[:, columns_of(pair, 2, INNER)]
    grads = gc_v[:, columns_of(pair, 0, INNER)]
    zero = jnp.zeros_like(grads)
    product_t = (grads.astype(F32) * context_v[:, columns_of(pair, 0, INNER)].astype(F32)).T
    key_grad = value_grad = None
    query_parts = []
    for half in range(2):
        rows = slice(half * HEAD_DIM, (half + 1) * HEAD_DIM)
        own = half_lanes(grads, half)
        probs = p_v[2 * pair + half]
        delta = jnp.sum(product_t[rows], axis=0, keepdims=True)
        weight_grad = dot_nt(jnp.where(own, values, zero), grads)
        score_grad = (probs.astype(F32) * (weight_grad - delta)).astype(BF16)
        key_part = dot_nn(score_grad, jnp.where(own, queries, zero))
        value_part = dot_nn(probs, jnp.where(own, grads, zero))
        key_grad = key_part if half == 0 else key_grad + key_part
        value_grad = value_part if half == 0 else value_grad + value_part
        query_parts.append(dot_nn(keys_t[rows], score_grad))
    grad_v[:, columns_of(pair, 0, INNER)] = jnp.concatenate(query_parts, axis=0).T.astype(BF16)
    grad_v[:, columns_of(pair, 1, INNER)] = key_grad.astype(BF16)
    grad_v[:, columns_of(pair, 2, INNER)] = value_grad.astype(BF16)


def input_gradient(upper_v, grad_v, x_v, w_v, gain_ref):
    grad_standard = dot_nt(grad_v[...], w_v[...]) * gain_ref[...]
    standard, inverse = statistics(x_v[...])
    correction = jnp.mean(grad_standard, axis=-1, keepdims=True) + standard * jnp.mean(
        grad_standard * standard, axis=-1, keepdims=True
    )
    return (upper_v[...].astype(F32) + inverse * (grad_standard - correction)).astype(BF16)


def section_body(layout, turn, aliased, with_input, *refs):
    gain_ref, received, top, x, qkv, weights, context = refs[:7]
    pieces, refs = zip_pieces(refs[7:], layout)
    refs = refs[aliased:]
    upper_out, grad_out, input_out = refs[:3] if with_input else (*refs[:2], None)
    refs = refs[3 if with_input else 2 :]
    upper_v, out_w, gc_v, grad_v, sems, w_sems = refs[:6]

    @pl.when(is_turn(turn))
    def _():
        w_copies = start_all(weight_copies(pieces, layout, out_w, w_sems, OUT_COLUMNS))
        top_copy = pltpu.make_async_copy(top, upper_v, sems.at[2])
        pl.when(is_top())(top_copy.start)

        @pl.when(jnp.logical_not(is_top()))
        def _():
            upper_v[...] = received[...]

        late = []
        if with_input:
            x_v, qkv_w, out_v, qkv_sems = refs[6:]
            late = weight_copies(pieces, layout, qkv_w, qkv_sems, QKV_COLUMNS)
            late.append(pltpu.make_async_copy(x, x_v, sems.at[3]))
        pl.when(is_top())(top_copy.wait)
        stores = start_all([pltpu.make_async_copy(upper_v, upper_out, sems.at[0])])
        wait_all(w_copies)
        start_all(late)
        gc_v[...] = dot_nn(upper_v[...], out_w[...]).astype(BF16)

        def one_pair(pair, unused):
            backward_pair(pair, qkv, weights, context, gc_v, grad_v)
            return unused

        lax.fori_loop(0, PAIRS, one_pair, 0, unroll=2)
        stores += start_all([pltpu.make_async_copy(grad_v, grad_out, sems.at[1])])
        if with_input:
            wait_all(late)
            out_v[...] = input_gradient(upper_v, grad_v, x_v, qkv_w, gain_ref)
            stores += start_all([pltpu.make_async_copy(out_v, input_out, sems.at[4])])
        wait_all(stores)


def section_backward(turn, with_input, gain, received, top, x, saved, gathered, layout, carry):
    length, width = x.shape
    weights, context, qkv = saved
    inputs = [gain, received, top, x, qkv, weights, context]
    specs = [VMEM, VMEM, ANY, ANY, VMEM, VMEM, VMEM]
    inputs = inputs + flat_pieces(gathered)
    outs = [shape((length, width)), shape((length, 3 * INNER))]
    outs = outs + [shape((length, width))] * with_input
    aliases = {}
    if carry is not None:
        aliases = {len(inputs) + index: index for index in range(len(outs))}
        inputs = inputs + list(carry[: len(outs)])

    def body(*refs):
        section_body(layout, turn, len(aliases), with_input, *refs)

    scratch = [
        pltpu.VMEM((length, width), BF16),
        pltpu.VMEM((width, INNER), BF16),
        pltpu.VMEM((length, INNER), BF16),
        pltpu.VMEM((length, 3 * INNER), BF16),
        pltpu.SemaphoreType.DMA((5,)),
        pltpu.SemaphoreType.DMA((copy_count(layout, OUT_COLUMNS),)),
    ]
    if with_input:
        scratch += [
            pltpu.VMEM((length, width), BF16),
            pltpu.VMEM((width, 3 * INNER), BF16),
            pltpu.VMEM((length, width), BF16),
            pltpu.SemaphoreType.DMA((copy_count(layout, QKV_COLUMNS),)),
        ]
    return call(
        body,
        tuple(outs),
        specs + [ANY] * (len(inputs) - len(specs)),
        (ANY,) * len(outs),
        scratch,
        24 if with_input else 16,
        aliases,
    )(*inputs)


def project_body(layout, turn, gain_ref, upper, grad, x, *refs):
    pieces, refs = zip_pieces(refs, layout)
    out, x_v, w_v, out_v, sems, w_sems = refs[1:]

    @pl.when(is_turn(turn))
    def _():
        copies = weight_copies(pieces, layout, w_v, w_sems, QKV_COLUMNS)
        copies.append(pltpu.make_async_copy(x, x_v, sems.at[0]))
        wait_all(start_all(copies))
        out_v[...] = input_gradient(upper, grad, x_v, w_v, gain_ref)
        wait_all(start_all([pltpu.make_async_copy(out_v, out, sems.at[1])]))


def project(turn, gain, upper, x, grad, gathered, layout, carry):
    length, width = x.shape
    inputs = [gain, upper, grad, x] + flat_pieces(gathered) + [carry]

    def body(*refs):
        project_body(layout, turn, *refs)

    return call(
        body,
        shape((length, width)),
        [VMEM] * 3 + [ANY] * (len(inputs) - 3),
        ANY,
        [
            pltpu.VMEM((length, width), BF16),
            pltpu.VMEM((width, 3 * INNER), BF16),
            pltpu.VMEM((length, width), BF16),
            pltpu.SemaphoreType.DMA((2,)),
            pltpu.SemaphoreType.DMA((copy_count(layout, QKV_COLUMNS),)),
        ],
        16,
        {len(inputs) - 1: 0},
    )(*inputs)


def term_body(layout, rows, normed, upper, grad, context, *refs):
    position = lax.axis_index("dp")
    count = 2 * len(layout[1])
    outs, (upper_t, normed_v, upper_v) = refs[:count], refs[count:]
    upper_t[...] = upper[...].T
    for chunk, (order, (start, stop)) in enumerate(zip(*layout)):
        half = len(order) // 2
        for slot, offset in enumerate(order):
            row = pl.multiple_of((position ^ offset) * rows, math.gcd(rows, 16))
            own, source = pl.ds(slot * rows, rows), pl.ds(row, rows)
            if start < 3 * INNER:
                normed_v[own] = normed[source]
            if stop > 3 * INNER:
                upper_v[own] = upper_t[source]
        for out, side in ((outs[2 * chunk + 1], 1), (outs[2 * chunk], 0)):
            at = slice(side * half * rows, (side + 1) * half * rows)

            def store(value, low, high, out=out):
                out[:, :, low - start : high - start] = value.astype(BF16).reshape(
                    half, rows, high - low
                )

            if start < 3 * INNER:
                high = min(stop, 3 * INNER)
                store(dot_nn(normed_v[at], grad[:, start:high]), start, high)
            if stop > 3 * INNER:
                low = max(start, 3 * INNER)
                part = context[:, low - 3 * INNER : stop - 3 * INNER]
                store(dot_nn(upper_v[at], part), low, stop)


def weight_terms(normed, upper, grad, context, rows, layout):
    width, length = normed.shape
    inputs = [normed, upper, grad, context]
    orders, columns = layout
    count = len(orders[0])
    outs = tuple(
        shape((count // 2, rows, stop - start)) for start, stop in columns for _ in range(2)
    )

    def body(*refs):
        term_body(layout, rows, *refs)

    return call(
        body,
        outs,
        [VMEM] * len(inputs),
        (VMEM,) * len(outs),
        [
            pltpu.VMEM((width, length), BF16),
            pltpu.VMEM((width, length), BF16),
            pltpu.VMEM((width, length), BF16),
        ],
        24,
    )(*inputs)


def bit_orders(count, free):
    bits = [1 << b for b in range(count.bit_length() - 1)]
    near, far = bits[:free], bits[free:][::-1]
    return [far + near[c:] + near[:c] for c in range(free)]


def slot_offsets(order):
    offsets = [0]
    for bit in order:
        offsets = offsets + [offset ^ bit for offset in offsets]
    return offsets


def exchange_layout(total, orders):
    wide = total // len(orders)
    columns = [(c * wide, (c + 1) * wide) for c in range(len(orders))]
    return [slot_offsets(order) for order in orders], columns


def across(value, bit):
    count = lax.axis_size("dp")
    return lax.ppermute(value, "dp", [(source, source ^ bit) for source in range(count)])


class Gather:
    def __init__(self, shard, orders):
        self.orders = orders
        self.steps = len(orders[0])
        self.layout = exchange_layout(shard.shape[1], orders)
        self.held = [shard[None]]
        self.step = 0
        self.final = None

    def advance(self):
        step, chunks = self.step, len(self.orders)
        if len(self.held) == 1 and len({order[step] for order in self.orders}) > 1:
            self.held = [self.held[0][:, :, start:stop] for start, stop in self.layout[1]]
        got = [across(held, order[step]) for held, order in zip(self.held, self.orders)]
        self.step = step + 1
        if self.step < self.steps:
            self.held = [jnp.concatenate(pair, axis=0) for pair in zip(self.held, got)]
        else:
            if len(got) < chunks:
                self.held = [self.held[0][:, :, start:stop] for start, stop in self.layout[1]]
                got = [got[0][:, :, start:stop] for start, stop in self.layout[1]]
            self.final = list(zip(self.held, got))

    def after(self, *values):
        self.held, values = lax.optimization_barrier((self.held, values))
        return values


def scatter_rows(terms, orders, scale):
    chunk_count = len(orders)
    steps = len(orders[0])
    kept = [[terms[2 * c]] for c in range(chunk_count)]
    outgoing = [terms[2 * c + 1] for c in range(chunk_count)]
    for step in reversed(range(steps)):
        if step == 0 and all(order[0] == orders[0][0] for order in orders):
            break
        got = [across(outgoing[c], orders[c][step]) for c in range(chunk_count)]
        for c in range(chunk_count):
            kept[c].append(got[c])
        if step:
            half = 1 << (step - 1)
            for c in range(chunk_count):
                total = sum(part[half : 2 * half].astype(F32) for part in kept[c])
                outgoing[c] = total.astype(BF16)
    total = jnp.concatenate(
        [sum(part[0].astype(F32) for part in kept[c]) for c in range(chunk_count)], axis=-1
    )
    if len(kept[0]) <= steps:
        last = across(jnp.concatenate([out[0] for out in outgoing], axis=-1), orders[0][0])
        total = total + last.astype(F32)
    return total * scale


def on_device(layer_input, saved_qkv, ln_gain, layer_weights, rand_blocks, out_grad):
    sections = lax.axis_size("pipe")
    replicas = lax.axis_size("dp")
    x, qkv, top, shard = layer_input[0, 0], saved_qkv[0, 0], out_grad[0], layer_weights[0]
    rand = rand_blocks[0]
    rows, total = shard.shape

    orders = bit_orders(replicas, 3)
    gather = Gather(shard, orders)
    saved = forward((0, PAIRS), rand, qkv, None)
    saved = gather.after(*saved)
    gather.advance()
    share = PAIRS // 3
    for part in range(3):
        saved = forward((part * share, share), rand, qkv, saved)
        if part == 0:
            normed = normed_transposed(x, ln_gain)
            *saved, normed = gather.after(*saved, normed)
            gather.advance()
        elif part == 1:
            gather.advance()
            saved = gather.after(*saved)
            gather.advance()
    while gather.final is None:
        gather.advance()
    pieces = (gather.final, gather.layout)

    received = top
    carry = None
    for turn in range(sections):
        below = turn + 1 < sections
        kept = section_backward(turn, below, ln_gain, received, top, x, saved, *pieces, carry)
        carry = [*kept, *(carry or kept)[len(kept) :]]
        if below:
            received = lax.ppermute(
                carry[2], "pipe", [(source, source - 1) for source in range(1, sections)]
            )
    upper, grad, grad_input = carry
    terms = weight_terms(
        normed, upper, grad, saved[1], rows, exchange_layout(total, orders)
    )
    summed = scatter_rows(terms, orders, 1.0 / replicas)
    grad_input = project(sections - 1, ln_gain, upper, x, grad, *pieces, grad_input)
    return (grad_input[None, None], summed[None])


def solution(mesh):
    placed = (
        P("pipe", "dp", None, None),
        P("pipe", "dp", None, None),
        P("pipe", None),
        P("pipe", "dp", None),
        P("pipe", None, None, None),
        P("dp", None, None),
    )
    return jax.shard_map(
        on_device,
        mesh=mesh,
        in_specs=placed,
        out_specs=(P("pipe", "dp", None, None), P("pipe", "dp", None)),
        check_vma=False,
    )
```

```python
import math

import jax
import jax.numpy as jnp
from jax import lax
from jax.experimental import pallas as pl
from jax.experimental.pallas import tpu as pltpu
from jax.sharding import PartitionSpec as P

HEADS = 12
HEAD_DIM = 64
BLOCK = 64
INNER = HEADS * HEAD_DIM
PAIR = 2 * HEAD_DIM
PAIRS = HEADS // 2
EPSILON = 1e-05
NEGATIVE = -1e30
SCALE = HEAD_DIM ** (-0.5)
QKV_COLUMNS = (0, 3 * INNER)
OUT_COLUMNS = (3 * INNER, 4 * INNER)
MEGABYTE = 1024 * 1024
F32 = jnp.float32
BF16 = jnp.bfloat16
ANY = pl.BlockSpec(memory_space=pl.ANY)
SMEM = pl.BlockSpec(memory_space=pltpu.SMEM)
HBM = pl.BlockSpec(memory_space=pltpu.HBM)
VMEM = pl.BlockSpec(memory_space=pltpu.VMEM)


def dot_nn(left, right):
    return lax.dot_general(left, right, (((1,), (0,)), ((), ())), preferred_element_type=F32)


def dot_nt(left, right):
    return lax.dot_general(left, right, (((1,), (1,)), ((), ())), preferred_element_type=F32)


def dot_tn(left, right):
    return lax.dot_general(left, right, (((0,), (0,)), ((), ())), preferred_element_type=F32)


def call(body, out_shape, in_specs, out_specs, scratch, megabytes, aliases=None):
    return pl.pallas_call(
        body,
        out_shape=out_shape,
        in_specs=in_specs,
        out_specs=out_specs,
        scratch_shapes=scratch,
        input_output_aliases=aliases or {},
        compiler_params=pltpu.CompilerParams(vmem_limit_bytes=megabytes * MEGABYTE),
    )


def shape(dims, dtype=BF16):
    return jax.ShapeDtypeStruct(dims, dtype)


def start_all(copies):
    for copy in copies:
        copy.start()
    return copies


def wait_all(copies):
    for copy in copies:
        copy.wait()


def scaled(value):
    return (value.astype(F32) * SCALE).astype(BF16)


def half_lanes(like, half):
    lane = lax.broadcasted_iota(jnp.int32, like.shape, 1)
    return (lane >= half * HEAD_DIM) & (lane < (half + 1) * HEAD_DIM)


def columns_of(pair, group, width):
    return pl.ds(pl.multiple_of(group * width + pair * PAIR, PAIR), PAIR)


def skipped_block(draws, middle, blocks):
    near = range(3, blocks - 1) if middle == 0 else range(1, blocks - 3)
    return sum(near) - jnp.sum(draws[middle : middle + 1], axis=1, keepdims=True)


def forward_pair(pair, index, width, rand_ref, qkv_v):
    queries = scaled(qkv_v[:, columns_of(index, 0, width)])
    keys = qkv_v[:, columns_of(index, 1, width)]
    values_t = qkv_v[:, columns_of(index, 2, width)].T
    blocks = queries.shape[0] // BLOCK
    row_block = lax.broadcasted_iota(jnp.int32, queries.shape, 0) // BLOCK
    lane = lax.broadcasted_iota(jnp.int32, queries.shape, 1)
    probs, parts = [], []
    for half in range(2):
        own = half_lanes(keys, half)
        low = skipped_block(rand_ref[2 * pair + half], 0, blocks)
        high = skipped_block(rand_ref[2 * pair + half], blocks - 3, blocks)
        first = (1 - half) * HEAD_DIM
        marks = ((lane == first) & (row_block == low)) | (
            (lane == first + 1) & (row_block == high)
        )
        bars = ((lane == first) & (row_block == 1)) | (
            (lane == first + 1) & (row_block == blocks - 2)
        )
        key_side = jnp.where(own, keys, jnp.where(marks, 1.0, 0.0).astype(BF16))
        query_side = jnp.where(own, queries, jnp.where(bars, NEGATIVE, 0.0).astype(BF16))
        scores = dot_nt(key_side, query_side)
        powers = jnp.exp(scores - jnp.max(scores, axis=0, keepdims=True))
        inverse = 1.0 / jnp.sum(powers, axis=0, keepdims=True)
        weights = (powers * inverse).astype(BF16)
        probs.append(weights)
        parts.append(dot_nn(values_t[half * HEAD_DIM : (half + 1) * HEAD_DIM], weights))
    return probs, jnp.concatenate(parts, axis=0).T.astype(BF16)


def is_top():
    return lax.axis_index("pipe") == lax.axis_size("pipe") - 1


def forward_body(pairs, aliased, rand_ref, qkv, *refs):
    @pl.when(is_top() if aliased else jnp.logical_not(is_top()))
    def _():
        forward_part(pairs, rand_ref, qkv, *refs[aliased:])


def forward_part(pairs, rand_ref, qkv, weights, context, kept, qkv_v, p_v, context_v, sems):
    first, count = pairs
    width = count * PAIR
    loads, stores = [], []
    for group in range(3):
        at = pl.ds(group * INNER + first * PAIR, width)
        held = qkv_v.at[:, pl.ds(group * width, width)]
        loads.append(pltpu.make_async_copy(qkv.at[:, at], held, sems.at[group]))
        stores.append(pltpu.make_async_copy(held, kept.at[:, at], sems.at[3 + group]))
    wait_all(start_all(loads))
    start_all(stores)

    def p_copy(index):
        held, at = pl.ds(2 * index, 2), pl.ds(2 * (first + index), 2)
        return pltpu.make_async_copy(p_v.at[held], weights.at[at], sems.at[7 + index])

    def one_pair(index, unused):
        probs, context_part = forward_pair(first + index, index, width, rand_ref, qkv_v)
        for half in range(2):
            p_v[2 * index + half] = probs[half]
        context_v[:, columns_of(index, 0, width)] = context_part
        p_copy(index).start()
        return unused

    lax.fori_loop(0, count, one_pair, 0)
    target = context.at[:, pl.ds(first * PAIR, width)]
    stores += start_all([pltpu.make_async_copy(context_v, target, sems.at[6])])
    stores += [p_copy(index) for index in range(count)]
    wait_all(stores)


def forward(pairs, rand, qkv, carry):
    first, count = pairs
    length = qkv.shape[0]
    carry = list(carry or ())
    aliases = {2 + index: index for index in range(len(carry))}

    def body(*refs):
        forward_body(pairs, len(carry), *refs)

    return call(
        body,
        (shape((HEADS, length, length)), shape((length, INNER)), shape((length, 3 * INNER))),
        [VMEM, HBM] + [ANY] * len(carry),
        (ANY,) * 3,
        [
            pltpu.VMEM((length, 3 * PAIR * count), BF16),
            pltpu.VMEM((2 * count, length, length), BF16),
            pltpu.VMEM((length, PAIR * count), BF16),
            pltpu.SemaphoreType.DMA((7 + count,)),
        ],
        22 if count > 2 else 14,
        aliases,
    )(rand, qkv, *carry)


def statistics(x):
    values = x.astype(F32)
    centred = values - jnp.mean(values, axis=-1, keepdims=True)
    inverse = lax.rsqrt(jnp.mean(centred * centred, axis=-1, keepdims=True) + EPSILON)
    return centred * inverse, inverse


def norm_body(x_ref, gain_ref, out_ref):
    standard, _ = statistics(x_ref[...])
    out_ref[...] = (standard * gain_ref[...]).astype(BF16).T


def normed_transposed(x, gain):
    length, width = x.shape
    return call(norm_body, shape((width, length)), [VMEM, VMEM], VMEM, [], 10)(x, gain)


def weight_copies(pieces, layout, target, sems, wanted):
    low, high = wanted
    position = lax.axis_index("dp")
    copies = []
    for (first, second), order, (start, stop) in zip(pieces, *layout):
        left, right = max(start, low), min(stop, high)
        if left >= right:
            continue
        half = first.shape[0]
        rows = first.shape[1]
        for slot, offset in enumerate(order):
            source = first if slot < half else second
            row = pl.multiple_of((position ^ offset) * rows, math.gcd(rows, 16))
            copies.append(
                pltpu.make_async_copy(
                    source.at[slot % half, :, pl.ds(left - start, right - left)],
                    target.at[pl.ds(row, rows), pl.ds(left - low, right - left)],
                    sems.at[len(copies)],
                )
            )
    return copies


def copy_count(layout, wanted):
    return sum(
        len(order)
        for order, (start, stop) in zip(*layout)
        if max(start, wanted[0]) < min(stop, wanted[1])
    )


def is_turn(turn):
    return lax.axis_index("pipe") == lax.axis_size("pipe") - 1 - turn


def zip_pieces(refs, layout):
    count = 2 * len(layout[1])
    return list(zip(refs[:count:2], refs[1:count:2])), refs[count:]


def flat_pieces(gathered):
    return [piece for pair in gathered for piece in pair]


def backward_pair(pair, qkv_v, p_v, context_v, gc_v, grad_v):
    queries = scaled(qkv_v[:, columns_of(pair, 0, INNER)])
    keys_t = scaled(qkv_v[:, columns_of(pair, 1, INNER)]).T
    values = qkv_v[:, columns_of(pair, 2, INNER)]
    grads = gc_v[:, columns_of(pair, 0, INNER)]
    zero = jnp.zeros_like(grads)
    product_t = (grads.astype(F32) * context_v[:, columns_of(pair, 0, INNER)].astype(F32)).T
    key_grad = value_grad = None
    query_parts = []
    for half in range(2):
        rows = slice(half * HEAD_DIM, (half + 1) * HEAD_DIM)
        own = half_lanes(grads, half)
        probs = p_v[2 * pair + half]
        delta = jnp.sum(product_t[rows], axis=0, keepdims=True)
        weight_grad = dot_nt(jnp.where(own, values, zero), grads)
        score_grad = (probs.astype(F32) * (weight_grad - delta)).astype(BF16)
        key_part = dot_nn(score_grad, jnp.where(own, queries, zero))
        value_part = dot_nn(probs, jnp.where(own, grads, zero))
        key_grad = key_part if half == 0 else key_grad + key_part
        value_grad = value_part if half == 0 else value_grad + value_part
        query_parts.append(dot_nn(keys_t[rows], score_grad))
    grad_v[:, columns_of(pair, 0, INNER)] = jnp.concatenate(query_parts, axis=0).T.astype(BF16)
    grad_v[:, columns_of(pair, 1, INNER)] = key_grad.astype(BF16)
    grad_v[:, columns_of(pair, 2, INNER)] = value_grad.astype(BF16)


def input_gradient(upper_v, grad_v, x_v, w_v, gain_ref):
    grad_standard = dot_nt(grad_v[...], w_v[...]) * gain_ref[...]
    standard, inverse = statistics(x_v[...])
    correction = jnp.mean(grad_standard, axis=-1, keepdims=True) + standard * jnp.mean(
        grad_standard * standard, axis=-1, keepdims=True
    )
    return (upper_v[...].astype(F32) + inverse * (grad_standard - correction)).astype(BF16)


def section_body(layout, turn, aliased, with_input, *refs):
    gain_ref, received, top, x, qkv, weights, context = refs[:7]
    pieces, refs = zip_pieces(refs[7:], layout)
    refs = refs[aliased:]
    upper_out, grad_out, input_out = refs[:3] if with_input else (*refs[:2], None)
    refs = refs[3 if with_input else 2 :]
    upper_v, out_w, gc_v, grad_v, sems, w_sems = refs[:6]

    @pl.when(is_turn(turn))
    def _():
        w_copies = start_all(weight_copies(pieces, layout, out_w, w_sems, OUT_COLUMNS))
        top_copy = pltpu.make_async_copy(top, upper_v, sems.at[2])
        pl.when(is_top())(top_copy.start)

        @pl.when(jnp.logical_not(is_top()))
        def _():
            upper_v[...] = received[...]

        late = []
        if with_input:
            x_v, qkv_w, out_v, qkv_sems = refs[6:]
            late = weight_copies(pieces, layout, qkv_w, qkv_sems, QKV_COLUMNS)
            late.append(pltpu.make_async_copy(x, x_v, sems.at[3]))
        pl.when(is_top())(top_copy.wait)
        stores = start_all([pltpu.make_async_copy(upper_v, upper_out, sems.at[0])])
        wait_all(w_copies)
        start_all(late)
        gc_v[...] = dot_nn(upper_v[...], out_w[...]).astype(BF16)

        def one_pair(pair, unused):
            backward_pair(pair, qkv, weights, context, gc_v, grad_v)
            return unused

        lax.fori_loop(0, PAIRS, one_pair, 0, unroll=2)
        stores += start_all([pltpu.make_async_copy(grad_v, grad_out, sems.at[1])])
        if with_input:
            wait_all(late)
            out_v[...] = input_gradient(upper_v, grad_v, x_v, qkv_w, gain_ref)
            stores += start_all([pltpu.make_async_copy(out_v, input_out, sems.at[4])])
        wait_all(stores)


def section_backward(turn, with_input, gain, received, top, x, saved, gathered, layout, carry):
    length, width = x.shape
    weights, context, qkv = saved
    inputs = [gain, received, top, x, qkv, weights, context]
    specs = [VMEM, VMEM, ANY, ANY, VMEM, VMEM, VMEM]
    inputs = inputs + flat_pieces(gathered)
    outs = [shape((length, width)), shape((length, 3 * INNER))]
    outs = outs + [shape((length, width))] * with_input
    aliases = {}
    if carry is not None:
        aliases = {len(inputs) + index: index for index in range(len(outs))}
        inputs = inputs + list(carry[: len(outs)])

    def body(*refs):
        section_body(layout, turn, len(aliases), with_input, *refs)

    scratch = [
        pltpu.VMEM((length, width), BF16),
        pltpu.VMEM((width, INNER), BF16),
        pltpu.VMEM((length, INNER), BF16),
        pltpu.VMEM((length, 3 * INNER), BF16),
        pltpu.SemaphoreType.DMA((5,)),
        pltpu.SemaphoreType.DMA((copy_count(layout, OUT_COLUMNS),)),
    ]
    if with_input:
        scratch += [
            pltpu.VMEM((length, width), BF16),
            pltpu.VMEM((width, 3 * INNER), BF16),
            pltpu.VMEM((length, width), BF16),
            pltpu.SemaphoreType.DMA((copy_count(layout, QKV_COLUMNS),)),
        ]
    return call(
        body,
        tuple(outs),
        specs + [ANY] * (len(inputs) - len(specs)),
        (ANY,) * len(outs),
        scratch,
        24 if with_input else 16,
        aliases,
    )(*inputs)


def project_body(layout, turn, gain_ref, upper, grad, x, *refs):
    pieces, refs = zip_pieces(refs, layout)
    out, x_v, w_v, out_v, sems, w_sems = refs[1:]

    @pl.when(is_turn(turn))
    def _():
        copies = weight_copies(pieces, layout, w_v, w_sems, QKV_COLUMNS)
        copies.append(pltpu.make_async_copy(x, x_v, sems.at[0]))
        wait_all(start_all(copies))
        out_v[...] = input_gradient(upper, grad, x_v, w_v, gain_ref)
        wait_all(start_all([pltpu.make_async_copy(out_v, out, sems.at[1])]))


def project(turn, gain, upper, x, grad, gathered, layout, carry):
    length, width = x.shape
    inputs = [gain, upper, grad, x] + flat_pieces(gathered) + [carry]

    def body(*refs):
        project_body(layout, turn, *refs)

    return call(
        body,
        shape((length, width)),
        [VMEM] * 3 + [ANY] * (len(inputs) - 3),
        ANY,
        [
            pltpu.VMEM((length, width), BF16),
            pltpu.VMEM((width, 3 * INNER), BF16),
            pltpu.VMEM((length, width), BF16),
            pltpu.SemaphoreType.DMA((2,)),
            pltpu.SemaphoreType.DMA((copy_count(layout, QKV_COLUMNS),)),
        ],
        16,
        {len(inputs) - 1: 0},
    )(*inputs)


def term_body(layout, rows, normed, upper, grad, context, *refs):
    position = lax.axis_index("dp")
    count = 2 * len(layout[1])
    outs, (upper_t, normed_v, upper_v) = refs[:count], refs[count:]
    upper_t[...] = upper[...].T
    for chunk, (order, (start, stop)) in enumerate(zip(*layout)):
        half = len(order) // 2
        for slot, offset in enumerate(order):
            row = pl.multiple_of((position ^ offset) * rows, math.gcd(rows, 16))
            own, source = pl.ds(slot * rows, rows), pl.ds(row, rows)
            if start < 3 * INNER:
                normed_v[own] = normed[source]
            if stop > 3 * INNER:
                upper_v[own] = upper_t[source]
        for out, side in ((outs[2 * chunk + 1], 1), (outs[2 * chunk], 0)):
            at = slice(side * half * rows, (side + 1) * half * rows)

            def store(value, low, high, out=out):
                out[:, :, low - start : high - start] = value.astype(BF16).reshape(
                    half, rows, high - low
                )

            if start < 3 * INNER:
                high = min(stop, 3 * INNER)
                store(dot_nn(normed_v[at], grad[:, start:high]), start, high)
            if stop > 3 * INNER:
                low = max(start, 3 * INNER)
                part = context[:, low - 3 * INNER : stop - 3 * INNER]
                store(dot_nn(upper_v[at], part), low, stop)


def weight_terms(normed, upper, grad, context, rows, layout):
    width, length = normed.shape
    inputs = [normed, upper, grad, context]
    orders, columns = layout
    count = len(orders[0])
    outs = tuple(
        shape((count // 2, rows, stop - start)) for start, stop in columns for _ in range(2)
    )

    def body(*refs):
        term_body(layout, rows, *refs)

    return call(
        body,
        outs,
        [VMEM] * len(inputs),
        (VMEM,) * len(outs),
        [
            pltpu.VMEM((width, length), BF16),
            pltpu.VMEM((width, length), BF16),
            pltpu.VMEM((width, length), BF16),
        ],
        24,
    )(*inputs)


def bit_orders(count, free):
    bits = [1 << b for b in range(count.bit_length() - 1)]
    near, far = bits[:free], bits[free:][::-1]
    return [far + near[c:] + near[:c] for c in range(free)]


def slot_offsets(order):
    offsets = [0]
    for bit in order:
        offsets = offsets + [offset ^ bit for offset in offsets]
    return offsets


def exchange_layout(total, orders):
    wide = total // len(orders)
    columns = [(c * wide, (c + 1) * wide) for c in range(len(orders))]
    return [slot_offsets(order) for order in orders], columns


def across(value, bit):
    count = lax.axis_size("dp")
    return lax.ppermute(value, "dp", [(source, source ^ bit) for source in range(count)])


class Gather:
    def __init__(self, shard, orders):
        self.orders = orders
        self.steps = len(orders[0])
        self.layout = exchange_layout(shard.shape[1], orders)
        self.held = [shard[None]]
        self.step = 0
        self.final = None

    def advance(self):
        step, chunks = self.step, len(self.orders)
        if len(self.held) == 1 and len({order[step] for order in self.orders}) > 1:
            self.held = [self.held[0][:, :, start:stop] for start, stop in self.layout[1]]
        got = [across(held, order[step]) for held, order in zip(self.held, self.orders)]
        self.step = step + 1
        if self.step < self.steps:
            self.held = [jnp.concatenate(pair, axis=0) for pair in zip(self.held, got)]
        else:
            if len(got) < chunks:
                self.held = [self.held[0][:, :, start:stop] for start, stop in self.layout[1]]
                got = [got[0][:, :, start:stop] for start, stop in self.layout[1]]
            self.final = list(zip(self.held, got))

    def after(self, *values):
        self.held, values = lax.optimization_barrier((self.held, values))
        return values


def scatter_rows(terms, orders, scale):
    chunk_count = len(orders)
    steps = len(orders[0])
    kept = [[terms[2 * c]] for c in range(chunk_count)]
    outgoing = [terms[2 * c + 1] for c in range(chunk_count)]
    for step in reversed(range(steps)):
        got = [across(outgoing[c], orders[c][step]) for c in range(chunk_count)]
        for c in range(chunk_count):
            kept[c].append(got[c])
        if step:
            half = 1 << (step - 1)
            for c in range(chunk_count):
                total = sum(part[half : 2 * half].astype(F32) for part in kept[c])
                outgoing[c] = total.astype(BF16)
    total = jnp.concatenate(
        [sum(part[0].astype(F32) for part in kept[c]) for c in range(chunk_count)], axis=-1
    )
    if len(kept[0]) <= steps:
        last = across(jnp.concatenate([out[0] for out in outgoing], axis=-1), orders[0][0])
        total = total + last.astype(F32)
    return total * scale


def on_device(layer_input, saved_qkv, ln_gain, layer_weights, rand_blocks, out_grad):
    sections = lax.axis_size("pipe")
    replicas = lax.axis_size("dp")
    x, qkv, top, shard = layer_input[0, 0], saved_qkv[0, 0], out_grad[0], layer_weights[0]
    rand = rand_blocks[0]
    rows, total = shard.shape

    orders = bit_orders(replicas, 3)
    gather = Gather(shard, orders)
    early = pltpu.with_memory_space_constraint(qkv, pltpu.HBM)
    saved = forward((0, PAIRS), rand, early, None)
    saved = gather.after(*saved)
    gather.advance()
    share = PAIRS // 3
    for part in range(3):
        saved = forward((part * share, share), rand, qkv, saved)
        if part == 0:
            normed = normed_transposed(x, ln_gain)
            *saved, normed = gather.after(*saved, normed)
            gather.advance()
        elif part == 1:
            gather.advance()
            saved = gather.after(*saved)
            gather.advance()
    while gather.final is None:
        gather.advance()
    pieces = (gather.final, gather.layout)

    received = top
    carry = None
    for turn in range(sections):
        below = turn + 1 < sections
        kept = section_backward(turn, below, ln_gain, received, top, x, saved, *pieces, carry)
        carry = [*kept, *(carry or kept)[len(kept) :]]
        if below:
            received = lax.ppermute(
                carry[2], "pipe", [(source, source - 1) for source in range(1, sections)]
            )
    upper, grad, grad_input = carry
    terms = weight_terms(
        normed, upper, grad, saved[1], rows, exchange_layout(total, orders)
    )
    summed = scatter_rows(terms, orders, 1.0 / replicas)
    grad_input = project(sections - 1, ln_gain, upper, x, grad, *pieces, grad_input)
    return (grad_input[None, None], summed[None])


def solution(mesh):
    placed = (
        P("pipe", "dp", None, None),
        P("pipe", "dp", None, None),
        P("pipe", None),
        P("pipe", "dp", None),
        P("pipe", None, None, None),
        P("dp", None, None),
    )
    return jax.shard_map(
        on_device,
        mesh=mesh,
        in_specs=placed,
        out_specs=(P("pipe", "dp", None, None), P("pipe", "dp", None)),
        check_vma=False,
    )
```

```python
import math

import jax
import jax.numpy as jnp
from jax import lax
from jax.experimental import pallas as pl
from jax.experimental.pallas import tpu as pltpu
from jax.sharding import PartitionSpec as P

HEADS = 12
HEAD_DIM = 64
BLOCK = 64
INNER = HEADS * HEAD_DIM
PAIR = 2 * HEAD_DIM
PAIRS = HEADS // 2
EPSILON = 1e-05
NEGATIVE = -1e30
SCALE = HEAD_DIM ** (-0.5)
QKV_COLUMNS = (0, 3 * INNER)
OUT_COLUMNS = (3 * INNER, 4 * INNER)
MEGABYTE = 1024 * 1024
F32 = jnp.float32
BF16 = jnp.bfloat16
ANY = pl.BlockSpec(memory_space=pl.ANY)
SMEM = pl.BlockSpec(memory_space=pltpu.SMEM)
HBM = pl.BlockSpec(memory_space=pltpu.HBM)
VMEM = pl.BlockSpec(memory_space=pltpu.VMEM)


def dot_nn(left, right):
    return lax.dot_general(left, right, (((1,), (0,)), ((), ())), preferred_element_type=F32)


def dot_nt(left, right):
    return lax.dot_general(left, right, (((1,), (1,)), ((), ())), preferred_element_type=F32)


def dot_tn(left, right):
    return lax.dot_general(left, right, (((0,), (0,)), ((), ())), preferred_element_type=F32)


def call(body, out_shape, in_specs, out_specs, scratch, megabytes, aliases=None):
    return pl.pallas_call(
        body,
        out_shape=out_shape,
        in_specs=in_specs,
        out_specs=out_specs,
        scratch_shapes=scratch,
        input_output_aliases=aliases or {},
        compiler_params=pltpu.CompilerParams(vmem_limit_bytes=megabytes * MEGABYTE),
    )


def shape(dims, dtype=BF16):
    return jax.ShapeDtypeStruct(dims, dtype)


def start_all(copies):
    for copy in copies:
        copy.start()
    return copies


def wait_all(copies):
    for copy in copies:
        copy.wait()


def scaled(value):
    return (value.astype(F32) * SCALE).astype(BF16)


def half_lanes(like, half):
    lane = lax.broadcasted_iota(jnp.int32, like.shape, 1)
    return (lane >= half * HEAD_DIM) & (lane < (half + 1) * HEAD_DIM)


def columns_of(pair, group, width):
    return pl.ds(pl.multiple_of(group * width + pair * PAIR, PAIR), PAIR)


def skipped_block(draws, middle, blocks):
    near = range(3, blocks - 1) if middle == 0 else range(1, blocks - 3)
    return sum(near) - jnp.sum(draws[middle : middle + 1], axis=1, keepdims=True)


def forward_pair(pair, index, width, rand_ref, qkv_v):
    queries = scaled(qkv_v[:, columns_of(index, 0, width)])
    keys = qkv_v[:, columns_of(index, 1, width)]
    values_t = qkv_v[:, columns_of(index, 2, width)].T
    blocks = queries.shape[0] // BLOCK
    row_block = lax.broadcasted_iota(jnp.int32, queries.shape, 0) // BLOCK
    lane = lax.broadcasted_iota(jnp.int32, queries.shape, 1)
    probs, parts = [], []
    for half in range(2):
        own = half_lanes(keys, half)
        low = skipped_block(rand_ref[2 * pair + half], 0, blocks)
        high = skipped_block(rand_ref[2 * pair + half], blocks - 3, blocks)
        first = (1 - half) * HEAD_DIM
        marks = ((lane == first) & (row_block == low)) | (
            (lane == first + 1) & (row_block == high)
        )
        bars = ((lane == first) & (row_block == 1)) | (
            (lane == first + 1) & (row_block == blocks - 2)
        )
        key_side = jnp.where(own, keys, jnp.where(marks, 1.0, 0.0).astype(BF16))
        query_side = jnp.where(own, queries, jnp.where(bars, NEGATIVE, 0.0).astype(BF16))
        scores = dot_nt(key_side, query_side)
        powers = jnp.exp(scores - jnp.max(scores, axis=0, keepdims=True))
        inverse = 1.0 / jnp.sum(powers, axis=0, keepdims=True)
        weights = (powers * inverse).astype(BF16)
        probs.append(weights)
        parts.append(dot_nn(values_t[half * HEAD_DIM : (half + 1) * HEAD_DIM], weights))
    return probs, jnp.concatenate(parts, axis=0).T.astype(BF16)


def is_top():
    return lax.axis_index("pipe") == lax.axis_size("pipe") - 1


def forward_body(pairs, aliased, rand_ref, qkv, *refs):
    @pl.when(is_top() if aliased else jnp.logical_not(is_top()))
    def _():
        forward_part(pairs, rand_ref, qkv, *refs[aliased:])


def forward_part(pairs, rand_ref, qkv, weights, context, kept, qkv_v, p_v, context_v, sems):
    first, count = pairs
    width = count * PAIR
    loads, stores = [], []
    for group in range(3):
        at = pl.ds(group * INNER + first * PAIR, width)
        held = qkv_v.at[:, pl.ds(group * width, width)]
        loads.append(pltpu.make_async_copy(qkv.at[:, at], held, sems.at[group]))
        stores.append(pltpu.make_async_copy(held, kept.at[:, at], sems.at[3 + group]))
    wait_all(start_all(loads))
    start_all(stores)

    def p_copy(index):
        held, at = pl.ds(2 * index, 2), pl.ds(2 * (first + index), 2)
        return pltpu.make_async_copy(p_v.at[held], weights.at[at], sems.at[7 + index])

    def one_pair(index, unused):
        probs, context_part = forward_pair(first + index, index, width, rand_ref, qkv_v)
        for half in range(2):
            p_v[2 * index + half] = probs[half]
        context_v[:, columns_of(index, 0, width)] = context_part
        p_copy(index).start()
        return unused

    lax.fori_loop(0, count, one_pair, 0)
    target = context.at[:, pl.ds(first * PAIR, width)]
    stores += start_all([pltpu.make_async_copy(context_v, target, sems.at[6])])
    stores += [p_copy(index) for index in range(count)]
    wait_all(stores)


def forward(pairs, rand, qkv, carry):
    first, count = pairs
    length = qkv.shape[0]
    carry = list(carry or ())
    aliases = {2 + index: index for index in range(len(carry))}

    def body(*refs):
        forward_body(pairs, len(carry), *refs)

    return call(
        body,
        (shape((HEADS, length, length)), shape((length, INNER)), shape((length, 3 * INNER))),
        [VMEM, HBM] + [ANY] * len(carry),
        (ANY,) * 3,
        [
            pltpu.VMEM((length, 3 * PAIR * count), BF16),
            pltpu.VMEM((2 * count, length, length), BF16),
            pltpu.VMEM((length, PAIR * count), BF16),
            pltpu.SemaphoreType.DMA((7 + count,)),
        ],
        22 if count > 2 else 14,
        aliases,
    )(rand, qkv, *carry)


def statistics(x):
    values = x.astype(F32)
    centred = values - jnp.mean(values, axis=-1, keepdims=True)
    inverse = lax.rsqrt(jnp.mean(centred * centred, axis=-1, keepdims=True) + EPSILON)
    return centred * inverse, inverse


def norm_body(x_ref, gain_ref, out_ref):
    standard, _ = statistics(x_ref[...])
    out_ref[...] = (standard * gain_ref[...]).astype(BF16).T


def normed_transposed(x, gain):
    length, width = x.shape
    return call(norm_body, shape((width, length)), [VMEM, VMEM], VMEM, [], 10)(x, gain)


def weight_copies(pieces, layout, target, sems, wanted):
    low, high = wanted
    position = lax.axis_index("dp")
    copies = []
    for (first, second), order, (start, stop) in zip(pieces, *layout):
        left, right = max(start, low), min(stop, high)
        if left >= right:
            continue
        half = first.shape[0]
        rows = first.shape[1]
        for slot, offset in enumerate(order):
            source = first if slot < half else second
            row = pl.multiple_of((position ^ offset) * rows, math.gcd(rows, 16))
            copies.append(
                pltpu.make_async_copy(
                    source.at[slot % half, :, pl.ds(left - start, right - left)],
                    target.at[pl.ds(row, rows), pl.ds(left - low, right - left)],
                    sems.at[len(copies)],
                )
            )
    return copies


def copy_count(layout, wanted):
    return sum(
        len(order)
        for order, (start, stop) in zip(*layout)
        if max(start, wanted[0]) < min(stop, wanted[1])
    )


def is_turn(turn):
    return lax.axis_index("pipe") == lax.axis_size("pipe") - 1 - turn


def zip_pieces(refs, layout):
    count = 2 * len(layout[1])
    return list(zip(refs[:count:2], refs[1:count:2])), refs[count:]


def flat_pieces(gathered):
    return [piece for pair in gathered for piece in pair]


def backward_pair(pair, qkv_v, p_v, context_v, gc_v, grad_v):
    queries = scaled(qkv_v[:, columns_of(pair, 0, INNER)])
    keys_t = scaled(qkv_v[:, columns_of(pair, 1, INNER)]).T
    values = qkv_v[:, columns_of(pair, 2, INNER)]
    grads = gc_v[:, columns_of(pair, 0, INNER)]
    zero = jnp.zeros_like(grads)
    product_t = (grads.astype(F32) * context_v[:, columns_of(pair, 0, INNER)].astype(F32)).T
    key_grad = value_grad = None
    query_parts = []
    for half in range(2):
        rows = slice(half * HEAD_DIM, (half + 1) * HEAD_DIM)
        own = half_lanes(grads, half)
        probs = p_v[2 * pair + half]
        delta = jnp.sum(product_t[rows], axis=0, keepdims=True)
        weight_grad = dot_nt(jnp.where(own, values, zero), grads)
        score_grad = (probs.astype(F32) * (weight_grad - delta)).astype(BF16)
        key_part = dot_nn(score_grad, jnp.where(own, queries, zero))
        value_part = dot_nn(probs, jnp.where(own, grads, zero))
        key_grad = key_part if half == 0 else key_grad + key_part
        value_grad = value_part if half == 0 else value_grad + value_part
        query_parts.append(dot_nn(keys_t[rows], score_grad))
    grad_v[:, columns_of(pair, 0, INNER)] = jnp.concatenate(query_parts, axis=0).T.astype(BF16)
    grad_v[:, columns_of(pair, 1, INNER)] = key_grad.astype(BF16)
    grad_v[:, columns_of(pair, 2, INNER)] = value_grad.astype(BF16)


def input_gradient(upper_v, grad_v, x_v, w_v, gain_ref):
    grad_standard = dot_nt(grad_v[...], w_v[...]) * gain_ref[...]
    standard, inverse = statistics(x_v[...])
    correction = jnp.mean(grad_standard, axis=-1, keepdims=True) + standard * jnp.mean(
        grad_standard * standard, axis=-1, keepdims=True
    )
    return (upper_v[...].astype(F32) + inverse * (grad_standard - correction)).astype(BF16)


def assemble_body(layout, *refs):
    pieces, (out, sems) = zip_pieces(refs, layout)

    @pl.when(jnp.logical_not(is_top()))
    def _():
        wait_all(start_all(weight_copies(pieces, layout, out, sems, OUT_COLUMNS)))


def assemble(gathered, layout, width):
    inputs = flat_pieces(gathered)

    def body(*refs):
        assemble_body(layout, *refs)

    return call(
        body,
        shape((width, INNER)),
        [ANY] * len(inputs),
        ANY,
        [pltpu.SemaphoreType.DMA((copy_count(layout, OUT_COLUMNS),))],
        1,
    )(*inputs)


def section_body(layout, turn, aliased, with_input, *refs):
    gain_ref, received, top, x, qkv, weights, context, ready_w = refs[:8]
    pieces, refs = zip_pieces(refs[8:], layout)
    refs = refs[aliased:]
    upper_out, grad_out, input_out = refs[:3] if with_input else (*refs[:2], None)
    refs = refs[3 if with_input else 2 :]
    upper_v, out_w, gc_v, grad_v, sems, w_sems = refs[:6]
    if not with_input and not aliased:
        upper_v, grad_v = upper_out, grad_out

    @pl.when(is_turn(turn))
    def _():
        w_copies = []
        if turn == 0:
            w_copies = start_all(weight_copies(pieces, layout, out_w, w_sems, OUT_COLUMNS))
        top_copy = pltpu.make_async_copy(top, upper_v, sems.at[2])
        pl.when(is_top())(top_copy.start)

        @pl.when(jnp.logical_not(is_top()))
        def _():
            upper_v[...] = received[...]

        late = []
        if with_input:
            x_v, qkv_w, out_v, qkv_sems = refs[6:]
            late = weight_copies(pieces, layout, qkv_w, qkv_sems, QKV_COLUMNS)
            late.append(pltpu.make_async_copy(x, x_v, sems.at[3]))
        pl.when(is_top())(top_copy.wait)
        stores = []
        if upper_v is not upper_out:
            stores = start_all([pltpu.make_async_copy(upper_v, upper_out, sems.at[0])])
        wait_all(w_copies)
        start_all(late)
        projection = ready_w if turn else out_w
        gc_v[...] = dot_nn(upper_v[...], projection[...]).astype(BF16)

        def one_pair(pair, unused):
            backward_pair(pair, qkv, weights, context, gc_v, grad_v)
            return unused

        lax.fori_loop(0, PAIRS, one_pair, 0, unroll=2)
        if grad_v is not grad_out:
            stores += start_all([pltpu.make_async_copy(grad_v, grad_out, sems.at[1])])
        if with_input:
            wait_all(late)
            out_v[...] = input_gradient(upper_v, grad_v, x_v, qkv_w, gain_ref)
            stores += start_all([pltpu.make_async_copy(out_v, input_out, sems.at[4])])
        wait_all(stores)


def section_backward(
    turn, with_input, gain, received, top, x, saved, ready, gathered, layout, carry
):
    length, width = x.shape
    weights, context, qkv = saved
    inputs = [gain, received, top, x, qkv, weights, context, ready]
    specs = [VMEM, VMEM, ANY, ANY, VMEM, VMEM, VMEM, VMEM if turn else ANY]
    inputs = inputs + flat_pieces(gathered)
    outs = [shape((length, width)), shape((length, 3 * INNER))]
    outs = outs + [shape((length, width))] * with_input
    aliases = {}
    direct = turn == 1 and not with_input
    if carry is not None and not direct:
        aliases = {len(inputs) + index: index for index in range(len(outs))}
        inputs = inputs + list(carry[: len(outs)])

    def body(*refs):
        section_body(layout, turn, len(aliases), with_input, *refs)

    scratch = [
        pltpu.VMEM((length, width), BF16),
        pltpu.VMEM((width, INNER), BF16),
        pltpu.VMEM((length, INNER), BF16),
        pltpu.VMEM((length, 3 * INNER), BF16),
        pltpu.SemaphoreType.DMA((5,)),
        pltpu.SemaphoreType.DMA((copy_count(layout, OUT_COLUMNS),)),
    ]
    if with_input:
        scratch += [
            pltpu.VMEM((length, width), BF16),
            pltpu.VMEM((width, 3 * INNER), BF16),
            pltpu.VMEM((length, width), BF16),
            pltpu.SemaphoreType.DMA((copy_count(layout, QKV_COLUMNS),)),
        ]
    return call(
        body,
        tuple(outs),
        specs + [ANY] * (len(inputs) - len(specs)),
        (VMEM if direct else ANY,) * len(outs),
        scratch,
        24 if with_input else 16,
        aliases,
    )(*inputs)


def project_body(layout, turn, gain_ref, upper, grad, x, *refs):
    pieces, refs = zip_pieces(refs, layout)
    out, x_v, w_v, out_v, sems, w_sems = refs[1:]

    @pl.when(is_turn(turn))
    def _():
        copies = weight_copies(pieces, layout, w_v, w_sems, QKV_COLUMNS)
        copies.append(pltpu.make_async_copy(x, x_v, sems.at[0]))
        wait_all(start_all(copies))
        out_v[...] = input_gradient(upper, grad, x_v, w_v, gain_ref)
        wait_all(start_all([pltpu.make_async_copy(out_v, out, sems.at[1])]))


def project(turn, gain, upper, x, grad, gathered, layout, carry):
    length, width = x.shape
    inputs = [gain, upper, grad, x] + flat_pieces(gathered) + [carry]

    def body(*refs):
        project_body(layout, turn, *refs)

    return call(
        body,
        shape((length, width)),
        [VMEM] * 3 + [ANY] * (len(inputs) - 3),
        ANY,
        [
            pltpu.VMEM((length, width), BF16),
            pltpu.VMEM((width, 3 * INNER), BF16),
            pltpu.VMEM((length, width), BF16),
            pltpu.SemaphoreType.DMA((2,)),
            pltpu.SemaphoreType.DMA((copy_count(layout, QKV_COLUMNS),)),
        ],
        16,
        {len(inputs) - 1: 0},
    )(*inputs)


def fill_terms(layout, rows, operands, outs, scratch):
    normed, upper, grad, context = operands
    upper_t, normed_v, upper_v = scratch
    position = lax.axis_index("dp")
    upper_t[...] = upper[...].T
    for chunk, (order, (start, stop)) in enumerate(zip(*layout)):
        half = len(order) // 2
        for slot, offset in enumerate(order):
            row = pl.multiple_of((position ^ offset) * rows, math.gcd(rows, 16))
            own, source = pl.ds(slot * rows, rows), pl.ds(row, rows)
            if start < 3 * INNER:
                normed_v[own] = normed[source]
            if stop > 3 * INNER:
                upper_v[own] = upper_t[source]
        for side in (1, 0):
            out = outs[2 * chunk + side]
            at = slice(side * half * rows, (side + 1) * half * rows)

            def store(value, low, high, out=out):
                out[:, :, low - start : high - start] = value.astype(BF16).reshape(
                    half, rows, high - low
                )

            if start < 3 * INNER:
                high = min(stop, 3 * INNER)
                store(dot_nn(normed_v[at], grad[:, start:high]), start, high)
            if stop > 3 * INNER:
                low = max(start, 3 * INNER)
                part = context[:, low - 3 * INNER : stop - 3 * INNER]
                store(dot_nn(upper_v[at], part), low, stop)


def top_term_body(layout, rows, *refs):
    count = 2 * len(layout[1])

    @pl.when(is_top())
    def _():
        outs, scratch = refs[4 : 4 + count], refs[4 + count :]
        fill_terms(layout, rows, refs[:4], outs, scratch)


def lower_term_body(layout, rows, *refs):
    count = 2 * len(layout[1])
    kept, outs, scratch = refs[4 : 4 + count], refs[4 + count : 4 + 2 * count], refs[4 + 2 * count :]

    @pl.when(is_top())
    def _():
        for source, out in zip(kept, outs):
            out[...] = source[...]

    @pl.when(jnp.logical_not(is_top()))
    def _():
        fill_terms(layout, rows, refs[:4], outs, scratch)


def weight_terms(normed, upper, grad, context, rows, layout, carry):
    width, length = normed.shape
    orders, columns = layout
    count = len(orders[0])
    dims = [(count // 2, rows, stop - start) for start, stop in columns for _ in range(2)]
    inputs = [normed, upper, grad, context]
    scratch = [pltpu.VMEM((width, length), BF16)] * 3
    body = top_term_body
    if carry is not None:
        inputs = inputs + list(carry)
        body = lower_term_body

    def bound(*refs):
        body(layout, rows, *refs)

    return call(
        bound,
        tuple(shape(each) for each in dims),
        [VMEM] * len(inputs),
        (VMEM,) * len(dims),
        scratch,
        24,
    )(*inputs)


def bit_orders(count, free):
    bits = [1 << b for b in range(count.bit_length() - 1)]
    near, far = bits[:free], bits[free:][::-1]
    return [far + near[c:] + near[:c] for c in range(free)]


def scatter_orders(count, free):
    bits = [1 << b for b in range(count.bit_length() - 1)]
    near, far = bits[:free][::-1], bits[free:][::-1]
    return [far + near[-c:] + near[:-c] for c in range(free)]


def slot_offsets(order):
    offsets = [0]
    for bit in order:
        offsets = offsets + [offset ^ bit for offset in offsets]
    return offsets


def exchange_layout(total, orders):
    wide = total // len(orders)
    columns = [(c * wide, (c + 1) * wide) for c in range(len(orders))]
    return [slot_offsets(order) for order in orders], columns


def across(value, bit):
    count = lax.axis_size("dp")
    return lax.ppermute(value, "dp", [(source, source ^ bit) for source in range(count)])


class Gather:
    def __init__(self, shard, orders):
        self.orders = orders
        self.steps = len(orders[0])
        self.layout = exchange_layout(shard.shape[1], orders)
        self.held = [shard[None]]
        self.step = 0
        self.final = None

    def advance(self):
        step, chunks = self.step, len(self.orders)
        if len(self.held) == 1 and len({order[step] for order in self.orders}) > 1:
            self.held = [self.held[0][:, :, start:stop] for start, stop in self.layout[1]]
        got = [across(held, order[step]) for held, order in zip(self.held, self.orders)]
        self.step = step + 1
        if self.step < self.steps:
            self.held = [jnp.concatenate(pair, axis=0) for pair in zip(self.held, got)]
        else:
            if len(got) < chunks:
                self.held = [self.held[0][:, :, start:stop] for start, stop in self.layout[1]]
                got = [got[0][:, :, start:stop] for start, stop in self.layout[1]]
            self.final = list(zip(self.held, got))

    def after(self, *values):
        self.held, values = lax.optimization_barrier((self.held, values))
        return values


def scatter_rows(terms, orders, scale):
    chunk_count = len(orders)
    steps = len(orders[0])
    kept = [[terms[2 * c]] for c in range(chunk_count)]
    outgoing = [terms[2 * c + 1] for c in range(chunk_count)]
    for step in reversed(range(steps)):
        got = [across(outgoing[c], orders[c][step]) for c in range(chunk_count)]
        for c in range(chunk_count):
            kept[c].append(got[c])
        if step:
            half = 1 << (step - 1)
            for c in range(chunk_count):
                total = sum(part[half : 2 * half].astype(F32) for part in kept[c])
                outgoing[c] = total.astype(BF16)
    total = jnp.concatenate(
        [sum(part[0].astype(F32) for part in kept[c]) for c in range(chunk_count)], axis=-1
    )
    if len(kept[0]) <= steps:
        last = across(jnp.concatenate([out[0] for out in outgoing], axis=-1), orders[0][0])
        total = total + last.astype(F32)
    return total * scale


def on_device(layer_input, saved_qkv, ln_gain, layer_weights, rand_blocks, out_grad):
    sections = lax.axis_size("pipe")
    replicas = lax.axis_size("dp")
    x, qkv, top, shard = layer_input[0, 0], saved_qkv[0, 0], out_grad[0], layer_weights[0]
    rand = rand_blocks[0]
    rows, total = shard.shape

    orders = bit_orders(replicas, 3)
    gather = Gather(shard, orders)
    early = pltpu.with_memory_space_constraint(qkv, pltpu.HBM)
    saved = forward((0, PAIRS), rand, early, None)
    saved = gather.after(*saved)
    gather.advance()
    share = PAIRS // 3
    for part in range(3):
        saved = forward((part * share, share), rand, qkv, saved)
        if part == 0:
            normed = normed_transposed(x, ln_gain)
            *saved, normed = gather.after(*saved, normed)
            gather.advance()
        elif part == 1:
            gather.advance()
            saved = gather.after(*saved)
            gather.advance()
    while gather.final is None:
        gather.advance()
    pieces = (gather.final, gather.layout)

    ready = assemble(*pieces, x.shape[1])

    received = top
    carry = terms = None
    back = scatter_orders(replicas, 3)
    layout = exchange_layout(total, back)
    for turn in range(sections):
        below = turn + 1 < sections
        kept = section_backward(
            turn, below, ln_gain, received, top, x, saved, ready if turn else top, *pieces, carry
        )
        carry = [*kept, *(carry or kept)[len(kept) :]]
        if below:
            received = lax.ppermute(
                carry[2], "pipe", [(source, source - 1) for source in range(1, sections)]
            )
        if turn == 0:
            terms = weight_terms(normed, *carry[:2], saved[1], rows, layout, None)
    upper, grad, grad_input = carry
    terms = weight_terms(normed, upper, grad, saved[1], rows, layout, terms)
    summed = scatter_rows(terms, back, 1.0 / replicas)
    grad_input = project(sections - 1, ln_gain, upper, x, grad, *pieces, grad_input)
    return (grad_input[None, None], summed[None])


def solution(mesh):
    placed = (
        P("pipe", "dp", None, None),
        P("pipe", "dp", None, None),
        P("pipe", None),
        P("pipe", "dp", None),
        P("pipe", None, None, None),
        P("dp", None, None),
    )
    return jax.shard_map(
        on_device,
        mesh=mesh,
        in_specs=placed,
        out_specs=(P("pipe", "dp", None, None), P("pipe", "dp", None)),
        check_vma=False,
    )
```

```python
import math

import jax
import jax.numpy as jnp
from jax import lax
from jax.experimental import pallas as pl
from jax.experimental.pallas import tpu as pltpu
from jax.sharding import PartitionSpec as P

HEADS = 12
HEAD_DIM = 64
BLOCK = 64
INNER = HEADS * HEAD_DIM
PAIR = 2 * HEAD_DIM
PAIRS = HEADS // 2
EPSILON = 1e-05
NEGATIVE = -1e30
SCALE = HEAD_DIM ** (-0.5)
QKV_COLUMNS = (0, 3 * INNER)
OUT_COLUMNS = (3 * INNER, 4 * INNER)
MEGABYTE = 1024 * 1024
F32 = jnp.float32
BF16 = jnp.bfloat16
ANY = pl.BlockSpec(memory_space=pl.ANY)
SMEM = pl.BlockSpec(memory_space=pltpu.SMEM)
HBM = pl.BlockSpec(memory_space=pltpu.HBM)
VMEM = pl.BlockSpec(memory_space=pltpu.VMEM)


def dot_nn(left, right):
    return lax.dot_general(left, right, (((1,), (0,)), ((), ())), preferred_element_type=F32)


def dot_nt(left, right):
    return lax.dot_general(left, right, (((1,), (1,)), ((), ())), preferred_element_type=F32)


def dot_tn(left, right):
    return lax.dot_general(left, right, (((0,), (0,)), ((), ())), preferred_element_type=F32)


def call(body, out_shape, in_specs, out_specs, scratch, megabytes, aliases=None):
    return pl.pallas_call(
        body,
        out_shape=out_shape,
        in_specs=in_specs,
        out_specs=out_specs,
        scratch_shapes=scratch,
        input_output_aliases=aliases or {},
        compiler_params=pltpu.CompilerParams(vmem_limit_bytes=megabytes * MEGABYTE),
    )


def shape(dims, dtype=BF16):
    return jax.ShapeDtypeStruct(dims, dtype)


def start_all(copies):
    for copy in copies:
        copy.start()
    return copies


def wait_all(copies):
    for copy in copies:
        copy.wait()


def scaled(value):
    return (value.astype(F32) * SCALE).astype(BF16)


def half_lanes(like, half):
    lane = lax.broadcasted_iota(jnp.int32, like.shape, 1)
    return (lane >= half * HEAD_DIM) & (lane < (half + 1) * HEAD_DIM)


def columns_of(pair, group, width):
    return pl.ds(pl.multiple_of(group * width + pair * PAIR, PAIR), PAIR)


def skipped_block(draws, middle, blocks):
    near = range(3, blocks - 1) if middle == 0 else range(1, blocks - 3)
    return sum(near) - jnp.sum(draws[middle : middle + 1], axis=1, keepdims=True)


def forward_pair(pair, index, width, rand_ref, qkv_v):
    queries = scaled(qkv_v[:, columns_of(index, 0, width)])
    keys = qkv_v[:, columns_of(index, 1, width)]
    values_t = qkv_v[:, columns_of(index, 2, width)].T
    blocks = queries.shape[0] // BLOCK
    row_block = lax.broadcasted_iota(jnp.int32, queries.shape, 0) // BLOCK
    lane = lax.broadcasted_iota(jnp.int32, queries.shape, 1)
    probs, parts = [], []
    for half in range(2):
        own = half_lanes(keys, half)
        low = skipped_block(rand_ref[2 * pair + half], 0, blocks)
        high = skipped_block(rand_ref[2 * pair + half], blocks - 3, blocks)
        first = (1 - half) * HEAD_DIM
        marks = ((lane == first) & (row_block == low)) | (
            (lane == first + 1) & (row_block == high)
        )
        bars = ((lane == first) & (row_block == 1)) | (
            (lane == first + 1) & (row_block == blocks - 2)
        )
        key_side = jnp.where(own, keys, jnp.where(marks, 1.0, 0.0).astype(BF16))
        query_side = jnp.where(own, queries, jnp.where(bars, NEGATIVE, 0.0).astype(BF16))
        scores = dot_nt(key_side, query_side)
        powers = jnp.exp(scores - jnp.max(scores, axis=0, keepdims=True))
        inverse = 1.0 / jnp.sum(powers, axis=0, keepdims=True)
        weights = (powers * inverse).astype(BF16)
        probs.append(weights)
        parts.append(dot_nn(values_t[half * HEAD_DIM : (half + 1) * HEAD_DIM], weights))
    return probs, jnp.concatenate(parts, axis=0).T.astype(BF16)


def is_top():
    return lax.axis_index("pipe") == lax.axis_size("pipe") - 1


def forward_body(pairs, aliased, rand_ref, qkv, *refs):
    @pl.when(is_top() if aliased else jnp.logical_not(is_top()))
    def _():
        forward_part(pairs, rand_ref, qkv, *refs[aliased:])


def forward_part(pairs, rand_ref, qkv, weights, context, kept, qkv_v, p_v, context_v, sems):
    first, count = pairs
    width = count * PAIR
    loads, stores = [], []
    for group in range(3):
        at = pl.ds(group * INNER + first * PAIR, width)
        held = qkv_v.at[:, pl.ds(group * width, width)]
        loads.append(pltpu.make_async_copy(qkv.at[:, at], held, sems.at[group]))
        stores.append(pltpu.make_async_copy(held, kept.at[:, at], sems.at[3 + group]))
    wait_all(start_all(loads))
    start_all(stores)

    def p_copy(index):
        held, at = pl.ds(2 * index, 2), pl.ds(2 * (first + index), 2)
        return pltpu.make_async_copy(p_v.at[held], weights.at[at], sems.at[7 + index])

    def one_pair(index, unused):
        probs, context_part = forward_pair(first + index, index, width, rand_ref, qkv_v)
        for half in range(2):
            p_v[2 * index + half] = probs[half]
        context_v[:, columns_of(index, 0, width)] = context_part
        p_copy(index).start()
        return unused

    lax.fori_loop(0, count, one_pair, 0)
    target = context.at[:, pl.ds(first * PAIR, width)]
    stores += start_all([pltpu.make_async_copy(context_v, target, sems.at[6])])
    stores += [p_copy(index) for index in range(count)]
    wait_all(stores)


def forward(pairs, rand, qkv, carry):
    first, count = pairs
    length = qkv.shape[0]
    carry = list(carry or ())
    aliases = {2 + index: index for index in range(len(carry))}

    def body(*refs):
        forward_body(pairs, len(carry), *refs)

    return call(
        body,
        (shape((HEADS, length, length)), shape((length, INNER)), shape((length, 3 * INNER))),
        [VMEM, HBM] + [ANY] * len(carry),
        (ANY,) * 3,
        [
            pltpu.VMEM((length, 3 * PAIR * count), BF16),
            pltpu.VMEM((2 * count, length, length), BF16),
            pltpu.VMEM((length, PAIR * count), BF16),
            pltpu.SemaphoreType.DMA((7 + count,)),
        ],
        22 if count > 2 else 14,
        aliases,
    )(rand, qkv, *carry)


def statistics(x):
    values = x.astype(F32)
    centred = values - jnp.mean(values, axis=-1, keepdims=True)
    inverse = lax.rsqrt(jnp.mean(centred * centred, axis=-1, keepdims=True) + EPSILON)
    return centred * inverse, inverse


def norm_body(x_ref, gain_ref, out_ref):
    standard, _ = statistics(x_ref[...])
    out_ref[...] = (standard * gain_ref[...]).astype(BF16).T


def normed_transposed(x, gain):
    length, width = x.shape
    return call(norm_body, shape((width, length)), [VMEM, VMEM], VMEM, [], 10)(x, gain)


def weight_copies(pieces, layout, target, sems, wanted):
    low, high = wanted
    position = lax.axis_index("dp")
    copies = []
    for (first, second), order, (start, stop) in zip(pieces, *layout):
        left, right = max(start, low), min(stop, high)
        if left >= right:
            continue
        half = first.shape[0]
        rows = first.shape[1]
        for slot, offset in enumerate(order):
            source = first if slot < half else second
            row = pl.multiple_of((position ^ offset) * rows, math.gcd(rows, 16))
            copies.append(
                pltpu.make_async_copy(
                    source.at[slot % half, :, pl.ds(left - start, right - left)],
                    target.at[pl.ds(row, rows), pl.ds(left - low, right - left)],
                    sems.at[len(copies)],
                )
            )
    return copies


def copy_count(layout, wanted):
    return sum(
        len(order)
        for order, (start, stop) in zip(*layout)
        if max(start, wanted[0]) < min(stop, wanted[1])
    )


def is_turn(turn):
    return lax.axis_index("pipe") == lax.axis_size("pipe") - 1 - turn


def zip_pieces(refs, layout):
    count = 2 * len(layout[1])
    return list(zip(refs[:count:2], refs[1:count:2])), refs[count:]


def flat_pieces(gathered):
    return [piece for pair in gathered for piece in pair]


def backward_pair(pair, qkv_v, p_v, context_v, gc_v, grad_v):
    queries = scaled(qkv_v[:, columns_of(pair, 0, INNER)])
    keys_t = scaled(qkv_v[:, columns_of(pair, 1, INNER)]).T
    values = qkv_v[:, columns_of(pair, 2, INNER)]
    grads = gc_v[:, columns_of(pair, 0, INNER)]
    zero = jnp.zeros_like(grads)
    product_t = (grads.astype(F32) * context_v[:, columns_of(pair, 0, INNER)].astype(F32)).T
    key_grad = value_grad = None
    query_parts = []
    for half in range(2):
        rows = slice(half * HEAD_DIM, (half + 1) * HEAD_DIM)
        own = half_lanes(grads, half)
        probs = p_v[2 * pair + half]
        delta = jnp.sum(product_t[rows], axis=0, keepdims=True)
        weight_grad = dot_nt(jnp.where(own, values, zero), grads)
        score_grad = (probs.astype(F32) * (weight_grad - delta)).astype(BF16)
        key_part = dot_nn(score_grad, jnp.where(own, queries, zero))
        value_part = dot_nn(probs, jnp.where(own, grads, zero))
        key_grad = key_part if half == 0 else key_grad + key_part
        value_grad = value_part if half == 0 else value_grad + value_part
        query_parts.append(dot_nn(keys_t[rows], score_grad))
    grad_v[:, columns_of(pair, 0, INNER)] = jnp.concatenate(query_parts, axis=0).T.astype(BF16)
    grad_v[:, columns_of(pair, 1, INNER)] = key_grad.astype(BF16)
    grad_v[:, columns_of(pair, 2, INNER)] = value_grad.astype(BF16)


def input_gradient(upper_v, grad_v, standard, inverse, w_v, gain_ref):
    grad_standard = dot_nt(grad_v[...], w_v[...]) * gain_ref[...]
    correction = jnp.mean(grad_standard, axis=-1, keepdims=True) + standard * jnp.mean(
        grad_standard * standard, axis=-1, keepdims=True
    )
    return (upper_v[...].astype(F32) + inverse * (grad_standard - correction)).astype(BF16)


def assemble_body(layout, *refs):
    pieces, (out, sems) = zip_pieces(refs, layout)

    @pl.when(jnp.logical_not(is_top()))
    def _():
        wait_all(start_all(weight_copies(pieces, layout, out, sems, OUT_COLUMNS)))


def assemble(gathered, layout, width):
    inputs = flat_pieces(gathered)

    def body(*refs):
        assemble_body(layout, *refs)

    return call(
        body,
        shape((width, INNER)),
        [ANY] * len(inputs),
        ANY,
        [pltpu.SemaphoreType.DMA((copy_count(layout, OUT_COLUMNS),))],
        1,
    )(*inputs)


def section_body(layout, turn, aliased, with_input, *refs):
    gain_ref, received, top, x, qkv, weights, context, ready_w = refs[:8]
    pieces, refs = zip_pieces(refs[8:], layout)
    refs = refs[aliased:]
    upper_out, grad_out, input_out = refs[:3] if with_input else (*refs[:2], None)
    refs = refs[3 if with_input else 2 :]
    upper_v, out_w, gc_v, grad_v, sems, w_sems = refs[:6]
    if not with_input and not aliased:
        upper_v, grad_v = upper_out, grad_out

    @pl.when(is_turn(turn))
    def _():
        w_copies = []
        if turn == 0:
            w_copies = start_all(weight_copies(pieces, layout, out_w, w_sems, OUT_COLUMNS))
        top_copy = pltpu.make_async_copy(top, upper_v, sems.at[2])
        pl.when(is_top())(top_copy.start)

        @pl.when(jnp.logical_not(is_top()))
        def _():
            upper_v[...] = received[...]

        late = []
        if with_input:
            x_v, qkv_w, out_v, qkv_sems, standard_v, inverse_v = refs[6:]
            x_copy = pltpu.make_async_copy(x, x_v, sems.at[3])
            x_copy.start()
            late = weight_copies(pieces, layout, qkv_w, qkv_sems, QKV_COLUMNS)
        pl.when(is_top())(top_copy.wait)
        stores = []
        if upper_v is not upper_out:
            stores = start_all([pltpu.make_async_copy(upper_v, upper_out, sems.at[0])])
        if with_input:
            x_copy.wait()
            standard_v[...], inverse_v[...] = statistics(x_v[...])
        wait_all(w_copies)
        start_all(late)
        projection = ready_w if turn else out_w
        gc_v[...] = dot_nn(upper_v[...], projection[...]).astype(BF16)

        def one_pair(pair, unused):
            backward_pair(pair, qkv, weights, context, gc_v, grad_v)
            return unused

        lax.fori_loop(0, PAIRS, one_pair, 0, unroll=2)
        if grad_v is not grad_out:
            stores += start_all([pltpu.make_async_copy(grad_v, grad_out, sems.at[1])])
        if with_input:
            wait_all(late)
            out_v[...] = input_gradient(
                upper_v, grad_v, standard_v[...], inverse_v[...], qkv_w, gain_ref
            )
            stores += start_all([pltpu.make_async_copy(out_v, input_out, sems.at[4])])
        wait_all(stores)


def section_backward(
    turn, with_input, gain, received, top, x, saved, ready, gathered, layout, carry
):
    length, width = x.shape
    weights, context, qkv = saved
    inputs = [gain, received, top, x, qkv, weights, context, ready]
    specs = [VMEM, VMEM, ANY, ANY, VMEM, VMEM, VMEM, VMEM if turn else ANY]
    inputs = inputs + flat_pieces(gathered)
    outs = [shape((length, width)), shape((length, 3 * INNER))]
    outs = outs + [shape((length, width))] * with_input
    aliases = {}
    direct = turn == 1 and not with_input
    if carry is not None and not direct:
        aliases = {len(inputs) + index: index for index in range(len(outs))}
        inputs = inputs + list(carry[: len(outs)])

    def body(*refs):
        section_body(layout, turn, len(aliases), with_input, *refs)

    scratch = [
        pltpu.VMEM((length, width), BF16),
        pltpu.VMEM((width, INNER), BF16),
        pltpu.VMEM((length, INNER), BF16),
        pltpu.VMEM((length, 3 * INNER), BF16),
        pltpu.SemaphoreType.DMA((5,)),
        pltpu.SemaphoreType.DMA((copy_count(layout, OUT_COLUMNS),)),
    ]
    if with_input:
        scratch += [
            pltpu.VMEM((length, width), BF16),
            pltpu.VMEM((width, 3 * INNER), BF16),
            pltpu.VMEM((length, width), BF16),
            pltpu.SemaphoreType.DMA((copy_count(layout, QKV_COLUMNS),)),
            pltpu.VMEM((length, width), F32),
            pltpu.VMEM((length, 1), F32),
        ]
    return call(
        body,
        tuple(outs),
        specs + [ANY] * (len(inputs) - len(specs)),
        (VMEM if direct else ANY,) * len(outs),
        scratch,
        24 if with_input else 16,
        aliases,
    )(*inputs)


def project_body(layout, turn, gain_ref, upper, grad, x, *refs):
    pieces, refs = zip_pieces(refs, layout)
    out, x_v, w_v, out_v, sems, w_sems = refs[1:]

    @pl.when(is_turn(turn))
    def _():
        copies = weight_copies(pieces, layout, w_v, w_sems, QKV_COLUMNS)
        copies.append(pltpu.make_async_copy(x, x_v, sems.at[0]))
        wait_all(start_all(copies))
        out_v[...] = input_gradient(upper, grad, *statistics(x_v[...]), w_v, gain_ref)
        wait_all(start_all([pltpu.make_async_copy(out_v, out, sems.at[1])]))


def project(turn, gain, upper, x, grad, gathered, layout, carry):
    length, width = x.shape
    inputs = [gain, upper, grad, x] + flat_pieces(gathered) + [carry]

    def body(*refs):
        project_body(layout, turn, *refs)

    return call(
        body,
        shape((length, width)),
        [VMEM] * 3 + [ANY] * (len(inputs) - 3),
        ANY,
        [
            pltpu.VMEM((length, width), BF16),
            pltpu.VMEM((width, 3 * INNER), BF16),
            pltpu.VMEM((length, width), BF16),
            pltpu.SemaphoreType.DMA((2,)),
            pltpu.SemaphoreType.DMA((copy_count(layout, QKV_COLUMNS),)),
        ],
        16,
        {len(inputs) - 1: 0},
    )(*inputs)


def fill_terms(layout, rows, operands, outs, scratch):
    normed, upper, grad, context = operands
    upper_t, normed_v, upper_v = scratch
    position = lax.axis_index("dp")
    upper_t[...] = upper[...].T
    for chunk, (order, (start, stop)) in enumerate(zip(*layout)):
        half = len(order) // 2
        for slot, offset in enumerate(order):
            row = pl.multiple_of((position ^ offset) * rows, math.gcd(rows, 16))
            own, source = pl.ds(slot * rows, rows), pl.ds(row, rows)
            if start < 3 * INNER:
                normed_v[own] = normed[source]
            if stop > 3 * INNER:
                upper_v[own] = upper_t[source]
        for side in (1, 0):
            out = outs[2 * chunk + side]
            at = slice(side * half * rows, (side + 1) * half * rows)

            def store(value, low, high, out=out):
                out[:, :, low - start : high - start] = value.astype(BF16).reshape(
                    half, rows, high - low
                )

            if start < 3 * INNER:
                high = min(stop, 3 * INNER)
                store(dot_nn(normed_v[at], grad[:, start:high]), start, high)
            if stop > 3 * INNER:
                low = max(start, 3 * INNER)
                part = context[:, low - 3 * INNER : stop - 3 * INNER]
                store(dot_nn(upper_v[at], part), low, stop)


def top_term_body(layout, rows, *refs):
    count = 2 * len(layout[1])

    @pl.when(is_top())
    def _():
        outs, scratch = refs[4 : 4 + count], refs[4 + count :]
        fill_terms(layout, rows, refs[:4], outs, scratch)


def lower_term_body(layout, rows, *refs):
    count = 2 * len(layout[1])
    kept, outs, scratch = refs[4 : 4 + count], refs[4 + count : 4 + 2 * count], refs[4 + 2 * count :]

    @pl.when(is_top())
    def _():
        for source, out in zip(kept, outs):
            out[...] = source[...]

    @pl.when(jnp.logical_not(is_top()))
    def _():
        fill_terms(layout, rows, refs[:4], outs, scratch)


def weight_terms(normed, upper, grad, context, rows, layout, carry):
    width, length = normed.shape
    orders, columns = layout
    count = len(orders[0])
    dims = [(count // 2, rows, stop - start) for start, stop in columns for _ in range(2)]
    inputs = [normed, upper, grad, context]
    scratch = [pltpu.VMEM((width, length), BF16)] * 3
    body = top_term_body
    if carry is not None:
        inputs = inputs + list(carry)
        body = lower_term_body

    def bound(*refs):
        body(layout, rows, *refs)

    return call(
        bound,
        tuple(shape(each) for each in dims),
        [VMEM] * len(inputs),
        (VMEM,) * len(dims),
        scratch,
        24,
    )(*inputs)


def bit_orders(count, free):
    bits = [1 << b for b in range(count.bit_length() - 1)]
    near, far = bits[:free], bits[free:][::-1]
    return [far + near[c:] + near[:c] for c in range(free)]


def scatter_orders(count, free):
    bits = [1 << b for b in range(count.bit_length() - 1)]
    near, far = bits[:free][::-1], bits[free:][::-1]
    return [far + near[-c:] + near[:-c] for c in range(free)]


def slot_offsets(order):
    offsets = [0]
    for bit in order:
        offsets = offsets + [offset ^ bit for offset in offsets]
    return offsets


def exchange_layout(total, orders):
    wide = total // len(orders)
    columns = [(c * wide, (c + 1) * wide) for c in range(len(orders))]
    return [slot_offsets(order) for order in orders], columns


def across(value, bit):
    count = lax.axis_size("dp")
    return lax.ppermute(value, "dp", [(source, source ^ bit) for source in range(count)])


class Gather:
    def __init__(self, shard, orders):
        self.orders = orders
        self.steps = len(orders[0])
        self.layout = exchange_layout(shard.shape[1], orders)
        self.held = [shard[None]]
        self.step = 0
        self.final = None

    def advance(self):
        step, chunks = self.step, len(self.orders)
        if len(self.held) == 1 and len({order[step] for order in self.orders}) > 1:
            self.held = [self.held[0][:, :, start:stop] for start, stop in self.layout[1]]
        got = [across(held, order[step]) for held, order in zip(self.held, self.orders)]
        self.step = step + 1
        if self.step < self.steps:
            self.held = [jnp.concatenate(pair, axis=0) for pair in zip(self.held, got)]
        else:
            if len(got) < chunks:
                self.held = [self.held[0][:, :, start:stop] for start, stop in self.layout[1]]
                got = [got[0][:, :, start:stop] for start, stop in self.layout[1]]
            self.final = list(zip(self.held, got))

    def after(self, *values):
        self.held, values = lax.optimization_barrier((self.held, values))
        return values


def scatter_rows(terms, orders, scale):
    chunk_count = len(orders)
    steps = len(orders[0])
    kept = [[terms[2 * c]] for c in range(chunk_count)]
    outgoing = [terms[2 * c + 1] for c in range(chunk_count)]
    for step in reversed(range(steps)):
        got = [across(outgoing[c], orders[c][step]) for c in range(chunk_count)]
        for c in range(chunk_count):
            kept[c].append(got[c])
        if step:
            half = 1 << (step - 1)
            for c in range(chunk_count):
                total = sum(part[half : 2 * half].astype(F32) for part in kept[c])
                outgoing[c] = total.astype(BF16)
    total = jnp.concatenate(
        [sum(part[0].astype(F32) for part in kept[c]) for c in range(chunk_count)], axis=-1
    )
    if len(kept[0]) <= steps:
        last = across(jnp.concatenate([out[0] for out in outgoing], axis=-1), orders[0][0])
        total = total + last.astype(F32)
    return total * scale


def on_device(layer_input, saved_qkv, ln_gain, layer_weights, rand_blocks, out_grad):
    sections = lax.axis_size("pipe")
    replicas = lax.axis_size("dp")
    x, qkv, top, shard = layer_input[0, 0], saved_qkv[0, 0], out_grad[0], layer_weights[0]
    rand = rand_blocks[0]
    rows, total = shard.shape

    orders = bit_orders(replicas, 3)
    gather = Gather(shard, orders)
    early = pltpu.with_memory_space_constraint(qkv, pltpu.HBM)
    saved = forward((0, PAIRS), rand, early, None)
    saved = gather.after(*saved)
    gather.advance()
    share = PAIRS // 3
    for part in range(3):
        saved = forward((part * share, share), rand, qkv, saved)
        if part == 0:
            normed = normed_transposed(x, ln_gain)
            *saved, normed = gather.after(*saved, normed)
            gather.advance()
        elif part == 1:
            gather.advance()
            saved = gather.after(*saved)
            gather.advance()
    while gather.final is None:
        gather.advance()
    pieces = (gather.final, gather.layout)

    ready = assemble(*pieces, x.shape[1])

    received = top
    carry = terms = None
    back = scatter_orders(replicas, 3)
    layout = exchange_layout(total, back)
    for turn in range(sections):
        below = turn + 1 < sections
        kept = section_backward(
            turn, below, ln_gain, received, top, x, saved, ready if turn else top, *pieces, carry
        )
        carry = [*kept, *(carry or kept)[len(kept) :]]
        if below:
            received = lax.ppermute(
                carry[2], "pipe", [(source, source - 1) for source in range(1, sections)]
            )
        if turn == 0:
            terms = weight_terms(normed, *carry[:2], saved[1], rows, layout, None)
    upper, grad, grad_input = carry
    terms = weight_terms(normed, upper, grad, saved[1], rows, layout, terms)
    summed = scatter_rows(terms, back, 1.0 / replicas)
    grad_input = project(sections - 1, ln_gain, upper, x, grad, *pieces, grad_input)
    return (grad_input[None, None], summed[None])


def solution(mesh):
    placed = (
        P("pipe", "dp", None, None),
        P("pipe", "dp", None, None),
        P("pipe", None),
        P("pipe", "dp", None),
        P("pipe", None, None, None),
        P("dp", None, None),
    )
    return jax.shard_map(
        on_device,
        mesh=mesh,
        in_specs=placed,
        out_specs=(P("pipe", "dp", None, None), P("pipe", "dp", None)),
        check_vma=False,
    )
```
